1024 devices in a mesh: band: 32 (over z_lo, y), ga: 32 (over z_hi, x, core).
Axes of the slice: x: 4, y: 8, z: 16 (z_hi: 4, z_lo: 4; z = z_hi * 4 + z_lo), core: 2. Of those that a mesh axis runs over, the one named last changes fastest.
Arguments:
- valence: bfloat16 [32, 2, 128, 128, 128], P('band', None, 'ga'), may hold values from -6 to 6
- conduction: bfloat16 [192, 128, 128, 128], P('band', 'ga'), may hold values from -6 to 6
- owners: int32 [2], replicated, may hold values from 0 to 31
- val_energy: float32 [2], replicated, may hold values from -8 to -4
- cond_energy: float32 [192], P('band'), may hold values from 0.5 to 20
- gvec_index: int32 [10240], P('ga'), may hold values from 0 to 8191, as said below
Outputs:
- chi_panel: float32 [10240, 4096], P('band', 'ga')
The draws below stay inside these ranges and needn't reach their ends.
Inputs may be any that keep to these rules, and one draw needn't show every extreme that they name: owners[k] is the band group whose slot k holds valence band k. `gvec_index`: within each block j of 320 entries the values are distinct; value a 128 + b * 64 + c names x-frequency index a, y-frequency index j * 2 + b, z-frequency index c.
All inputs are finite; a program needn't handle non-finite values.
Results may differ from the reference program's by a relative error of at most 0.0048.
Values may be sent and summed in bfloat16 or wider, within the bound.
A program may use at most 32 MiB of HBM per device.

```python
import math
import jax
import jax.numpy as jnp
from jax import lax

NGRID = 128
KB = 64
NV = 2
NGD = 320
PANEL_DEV = 128
KYD = 2
GCELLS = 8192
NG = 10240
CBANDS = 192
N_BAND = 32
N_GA = 32


def draw_gvec_index(key, part):

    def one_block(block_key):
        inner = jax.random.permutation(jax.random.fold_in(block_key, 1), GCELLS - 2)[:NGD - 2] + 1
        ends = jnp.array([0, GCELLS - 1], dtype=jnp.int32)
        joined = jnp.concatenate([inner.astype(jnp.int32), ends])
        order = jax.random.permutation(jax.random.fold_in(block_key, 2), NGD)
        return joined[order]
    block_numbers = jnp.arange(NG // NGD)
    block_keys = jax.vmap(lambda number: jax.random.fold_in(key, number))(block_numbers)
    return jax.vmap(one_block)(block_keys).reshape(NG)


def block_levels(rng, shape, split, least, high):
    loudness = 1.0
    for dim, blocks in split:
        heights = jax.random.uniform(jax.random.fold_in(jax.random.fold_in(rng, 6), dim), (blocks,), jnp.float32, least / len(split), high / len(split))
        loudness = loudness * jnp.repeat(jnp.exp(heights), shape[dim] // blocks).reshape((-1,) + (1,) * (len(shape) - 1 - dim))
    return loudness


def gaussian(rng, extent, deviation, most, split=(), kind=jnp.bfloat16):
    values = deviation * jax.random.normal(rng, extent, jnp.float32)
    if split:
        values = values * block_levels(rng, extent, split, -0.22, 0.18)
    return jnp.clip(values, -most, most).astype(kind)


def setup_inputs(seed: int = 0) -> dict:
    streams_of = jax.random.split(jax.random.key(seed), 7)
    return {
        "valence": gaussian(streams_of[0], (N_BAND, NV, NGRID, NGRID, NGRID), 1.0, 6.0, ((0, 32), (2, 32))),
        "conduction": gaussian(streams_of[1], (CBANDS, NGRID, NGRID, NGRID), 1.0, 6.0, ((0, 32), (1, 32))),
        "owners": jax.random.randint(streams_of[2], (NV,), 0, N_BAND).astype(jnp.int32),
        "val_energy": jnp.clip(jax.random.uniform(streams_of[3], (NV,), jnp.float32, -8.0, -4.0), -8.0, -4.0),
        "cond_energy": jnp.clip(0.5 + 19.5 * jax.random.uniform(streams_of[4], (CBANDS,), jnp.float32) ** block_levels(streams_of[4], (CBANDS,), ((0, 32),), -0.2, 0.2), 0.5, 20.0),
        "gvec_index": draw_gvec_index(jax.random.fold_in(streams_of[6], 71), 0),
    }


highest = lax.Precision.HIGHEST

def dft_tables(grid_count, freq_count):
    grid_points = jnp.arange(grid_count, dtype=jnp.int32)
    shifted = jnp.arange(freq_count, dtype=jnp.int32) - freq_count // 2
    phase_index = grid_points[:, None] * shifted[None, :] % grid_count
    angles = phase_index.astype(jnp.float32) * (2.0 * math.pi / grid_count)
    scale_factor = 1.0 / math.sqrt(grid_count)
    return (jnp.cos(angles) * scale_factor, -jnp.sin(angles) * scale_factor)

def transform(fields):
    cosine_table, sine_table = dft_tables(NGRID, KB)
    both_tables = jnp.concatenate([cosine_table, sine_table], axis=1)
    zpart = jnp.einsum('vxyz,zq->vxyq', fields, both_tables, precision=highest)
    real_z, imag_z = (zpart[..., :KB], zpart[..., KB:])
    real_y = jnp.einsum('vxyk,yq->vxqk', real_z, cosine_table, precision=highest) - jnp.einsum('vxyk,yq->vxqk', imag_z, sine_table, precision=highest)
    imag_y = jnp.einsum('vxyk,yq->vxqk', imag_z, cosine_table, precision=highest) + jnp.einsum('vxyk,yq->vxqk', real_z, sine_table, precision=highest)
    real_x = jnp.einsum('vxjk,xq->vqjk', real_y, cosine_table, precision=highest) - jnp.einsum('vxjk,xq->vqjk', imag_y, sine_table, precision=highest)
    imag_x = jnp.einsum('vxjk,xq->vqjk', imag_y, cosine_table, precision=highest) + jnp.einsum('vxjk,xq->vqjk', real_y, sine_table, precision=highest)
    return jnp.stack([real_x, imag_x], axis=1)

def reference(valence, conduction, owners, val_energy, cond_energy, gvec_index):
    val_list = [valence[owners[slot], slot].astype(jnp.float32) for slot in range(NV)]
    val_fields = jnp.stack(val_list, axis=0)
    block_index = jnp.arange(NGD * N_GA, dtype=jnp.int32) // NGD
    x_freq = gvec_index // (KYD * KB)
    y_freq = block_index * KYD + gvec_index // KB % KYD
    z_freq = gvec_index % KB
    flat_index = (x_freq * KB * KB + y_freq * KB + z_freq).astype(jnp.int32)

    def one_band(band_wave):
        fields = val_fields * band_wave.astype(jnp.float32)[None]
        spectrum = transform(fields).reshape(NV, 2, KB * KB * KB)
        return spectrum[:, :, flat_index]
    coeffs = lax.map(one_band, conduction)
    coeff_rows = coeffs.reshape(-1, NGD * N_GA).astype(jnp.bfloat16)
    weights = 1.0 / (val_energy[None, :] - cond_energy[:, None])
    col_weights = jnp.repeat(weights.reshape(-1), 2)
    positions = jnp.arange(PANEL_DEV * N_GA, dtype=jnp.int32)
    panel_index = positions // PANEL_DEV * NGD + positions % PANEL_DEV
    chosen = coeff_rows[:, panel_index]
    weighted = (chosen.astype(jnp.float32) * col_weights[:, None]).astype(jnp.bfloat16)
    return lax.dot_general(coeff_rows, weighted, (((0,), (0,)), ((), ())), preferred_element_type=jnp.float32)
```

```python
import math

import jax
import jax.numpy as jnp
import numpy as np
from jax import lax
from jax.experimental import pallas as pl
from jax.experimental.pallas import tpu as pltpu
from jax.sharding import PartitionSpec as P

NGRID = 128
KB = 64
NV = 2
NC = 6
NF = NV * NC
NGD = 320
PANEL = 128
NB = 32
NGA = 32

F32 = jnp.float32
BF16 = jnp.bfloat16
MESH = pl.DeviceIdType.MESH
VMEM = pl.BlockSpec(memory_space=pltpu.VMEM)
SMEM = pl.BlockSpec(memory_space=pltpu.SMEM)


def split_table(table, terms):
    parts = []
    rest = table.astype(np.float32)
    for _ in range(terms):
        part = rest.astype(jnp.bfloat16)
        parts.append(part)
        rest = rest - part.astype(np.float32)
    return parts


def tables():
    n = np.arange(NGRID)[:, None]
    m = np.arange(KB)[None, :] - KB // 2
    angle = ((n * m) % NGRID).astype(np.float64) * (2.0 * math.pi / NGRID)
    scale = 1.0 / math.sqrt(NGRID)
    c = np.cos(angle) * scale
    s = -np.sin(angle) * scale
    zh, zl = split_table(np.concatenate([c, s, -s, c], axis=1), 2)
    ztab = np.stack([np.concatenate([zh, zh], axis=0), np.concatenate([zl, zl], axis=0)])
    yh, yl = split_table(np.concatenate([c.T, s.T], axis=1), 2)
    ytab = np.concatenate([yh, yl], axis=0)
    own = np.concatenate([c.reshape(NGA, 4, KB), s.reshape(NGA, 4, KB)], axis=1)
    parts = split_table(own, 3)
    xtab = np.concatenate(parts + [np.zeros_like(parts[0])], axis=1)
    return ztab, ytab, xtab


def spread_kernel(own_ref, val_ref, gv_ref, out_ref, gva_ref, masked, recv, ss, sr, gs, gr, vs, vr):
    b = lax.axis_index("band")
    a = lax.axis_index("ga")
    barrier = pltpu.get_barrier_semaphore()

    def greet(d, carry):
        pl.semaphore_signal(barrier, 1, device_id=(lax.rem(b + d, NB), a), device_id_type=MESH)
        pl.semaphore_signal(barrier, 1, device_id=(b, lax.rem(a + d, NGA)), device_id_type=MESH)
        return carry

    lax.fori_loop(1, NB, greet, 0)
    half = NB // NV
    for k in range(NV):
        flag = jnp.where(own_ref[k] == b, 1.0, 0.0).astype(F32)
        block = val_ref[k * half : (k + 1) * half].astype(F32)
        masked[k * half : (k + 1) * half] = (block * flag).astype(BF16)
    gva_ref[a] = gv_ref[...]
    pl.semaphore_wait(barrier, 2 * (NB - 1))

    def piece(p):
        return pltpu.make_async_remote_copy(
            masked.at[p], recv.at[b], ss.at[p], sr.at[b], device_id=(p, a), device_id_type=MESH
        )

    def piece_in(p):
        return pltpu.make_async_remote_copy(
            masked.at[p], recv.at[p], ss.at[p], sr.at[p], device_id=(p, a), device_id_type=MESH
        )

    def whole(p):
        return pltpu.make_async_remote_copy(
            out_ref.at[b], out_ref.at[b], gs.at[p], gr.at[b], device_id=(p, a), device_id_type=MESH
        )

    def whole_in(p):
        return pltpu.make_async_remote_copy(
            out_ref.at[b], out_ref.at[p], gs.at[p], gr.at[p], device_id=(p, a), device_id_type=MESH
        )

    def gvec(q):
        return pltpu.make_async_remote_copy(
            gv_ref, gva_ref.at[a], vs.at[q], vr.at[a], device_id=(b, q), device_id_type=MESH
        )

    def gvec_in(q):
        return pltpu.make_async_remote_copy(
            gv_ref, gva_ref.at[q], vs.at[q], vr.at[q], device_id=(b, q), device_id_type=MESH
        )

    def over_band(fn):
        lax.fori_loop(1, NB, lambda d, carry: (fn(lax.rem(b + d, NB)), carry)[1], 0)

    def over_ga(fn):
        lax.fori_loop(1, NGA, lambda d, carry: (fn(lax.rem(a + d, NGA)), carry)[1], 0)

    over_band(lambda p: piece(p).start())
    over_ga(lambda q: gvec(q).start())

    def add(d, total):
        p = lax.rem(b + NB - d, NB)
        piece_in(p).wait_recv()
        return total + recv[p].astype(F32)

    total = lax.fori_loop(1, NB, add, masked[b].astype(F32))
    out_ref[b] = total.astype(BF16)
    over_band(lambda p: whole(p).start())
    over_ga(lambda q: gvec_in(q).wait_recv())
    over_band(lambda p: whole_in(p).wait_recv())
    over_band(lambda p: piece(p).wait_send())
    over_band(lambda p: whole(p).wait_send())
    over_ga(lambda q: gvec(q).wait_send())


def dot(x, y):
    return jnp.dot(x, y, preferred_element_type=F32)


def split(x):
    high = x.astype(BF16)
    return high, (x - high.astype(F32)).astype(BF16)


def compute_kernel(me_ref, cond_ref, val_ref, gva_ref, zt_ref, yt_ref, xt_ref, p_ref, y_scr):
    zeros = jnp.zeros((4 * KB, 128), F32)
    for xl in range(4):
        y_scr[(xl * 16 + NF) * KB : (xl + 1) * 16 * KB, :] = zeros

    def field(f, carry):
        c = lax.div(f, NV)
        k = lax.rem(f, NV)
        pair = (cond_ref[c].astype(F32) * val_ref[k].astype(F32)).reshape(4 * NGRID, NGRID)
        hl = jnp.concatenate(split(pair), axis=1)
        z = dot(hl, zt_ref[0]) + dot(hl, zt_ref[1])
        for xl in range(4):
            part = z[xl * NGRID : (xl + 1) * NGRID]
            zh, zl = split(jnp.concatenate([part[:, :128], part[:, 128:]], axis=0))
            both = dot(yt_ref[...], zh)
            out = both[:KB] + (both[KB:] + dot(yt_ref[0:KB, :], zl))
            row = pl.multiple_of((xl * 16 + f) * KB, KB)
            y_scr[pl.ds(row, KB), :] = out
        return carry

    lax.fori_loop(0, NF, field, 0)
    xt = xt_ref[me_ref[0]]
    lane = lax.broadcasted_iota(jnp.int32, (64, 128), 1) < KB
    cell = lax.broadcasted_iota(jnp.int32, (128, NGD), 0)
    xcell = lax.broadcasted_iota(jnp.int32, (KB, NGD), 0)

    def block(j, carry):
        y0 = y_scr[pl.ds(2 * j, 64, stride=KB), :]
        y1 = y_scr[pl.ds(2 * j + 1, 64, stride=KB), :]
        ur = jnp.where(lane, y0, pltpu.roll(y1, KB, 1))
        ui = jnp.where(lane, pltpu.roll(y0, KB, 1), y1)
        hl = jnp.concatenate(split(jnp.concatenate([ur, ui], axis=0)), axis=1)
        v = gva_ref[j]
        hot = jnp.where(cell == (v & 127), 1.0, 0.0).astype(BF16)
        xhot = jnp.where(xcell == (v >> 7), 1.0, 0.0).astype(BF16)
        sel = dot(hl, jnp.concatenate([hot, hot], axis=0))
        e3 = dot(xt, xhot)
        e = e3[0:8] + (e3[8:16] + e3[16:24])
        re = jnp.zeros((16, NGD), F32)
        im = jnp.zeros((16, NGD), F32)
        for xl in range(4):
            sr = sel[xl * 16 : (xl + 1) * 16]
            si = sel[64 + xl * 16 : 64 + (xl + 1) * 16]
            er = e[xl : xl + 1]
            ei = e[4 + xl : 5 + xl]
            re = re + (sr * er - si * ei)
            im = im + (si * er + sr * ei)
        zh = lax.div(j, 8)
        x = lax.rem(lax.div(j, 2), 4)
        c = lax.rem(j, 2)
        p_ref[c, x, zh] = jnp.concatenate([re[:NF], im[:NF]], axis=0)
        return carry

    lax.fori_loop(0, NGA, block, 0)


def exchange_kernel(
    p_ref, w_ref, r_ref, wo_ref, c_rcv, s1, x_rcv, s2, z_rcv, pack, t_buf, w_buf,
    cs, cr, xs, xr, zs, zr, ts, tr, ps, pr, xas, xar, cas, car,
):
    b = lax.axis_index("band")
    a = lax.axis_index("ga")
    zl, y = lax.div(b, 8), lax.rem(b, 8)
    zh, x, c = lax.div(a, 8), lax.rem(lax.div(a, 2), 4), lax.rem(a, 2)
    e = lax.rem(a, 8)
    other = a + 1 - 2 * c
    barrier = pltpu.get_barrier_semaphore()

    def copy(src, dst, send, recv, where):
        return pltpu.make_async_remote_copy(
            src, dst, send, recv, device_id=where, device_id_type=MESH
        )

    def at_x(xx):
        return (b, zh * 8 + xx * 2 + c)

    def at_z(zz):
        return (b, zz * 8 + x * 2 + c)

    def greet(band, ga):
        pl.semaphore_signal(barrier, 1, device_id=(band, ga), device_id_type=MESH)

    greet(b, other)
    for d in range(1, 4):
        greet(*at_x(lax.rem(x + d, 4)))
        greet(*at_z(lax.rem(zh + d, 4)))
    for s in range(4):
        source = s * 8 + e

        @pl.when(jnp.logical_or(source != b, a != b))
        def _():
            greet(source, b)

    def greet_band(d, carry):
        greet(lax.rem(b + d, NB), a)
        return carry

    lax.fori_loop(1, NB, greet_band, 0)
    pl.semaphore_wait(barrier, 38 + 4 - jnp.where(a == b, 1, 0))

    order = [lax.rem(x + d, 4) for d in (1, 2, 3)] + [x]
    core = [copy(p_ref.at[1 - c, xx], c_rcv.at[xx], cs.at[xx], cr.at[xx], (b, other)) for xx in order]
    for op in core:
        op.start()
    x_ops = []
    for op, xx in zip(core, order):
        op.wait_recv()
        s1[xx] = p_ref[c, xx] + c_rcv[xx]
        if len(x_ops) < 3:
            go = copy(s1.at[xx], x_rcv.at[x], xs.at[xx], xr.at[x], at_x(xx))
            go.start()
            x_ops.append(go)
    for xx in order[:3]:
        copy(s1.at[xx], x_rcv.at[xx], xs.at[xx], xr.at[xx], at_x(xx)).wait_recv()
    z_order = [lax.rem(zh + d, 4) for d in (2, 1, 3)] + [zh]
    z_ops = []
    for zz in z_order:
        s2[zz] = (s1[x, zz] + x_rcv[order[0], zz]) + (x_rcv[order[1], zz] + x_rcv[order[2], zz])
        if len(z_ops) < 3:
            go = copy(s2.at[zz], z_rcv.at[zh], zs.at[zz], zr.at[zh], at_z(zz))
            go.start()
            z_ops.append(go)
    for zz in z_order[:3]:
        copy(s2.at[zz], z_rcv.at[zz], zs.at[zz], zr.at[zz], at_z(zz)).wait_recv()
    total = (s2[zh] + z_rcv[z_order[0]]) + (z_rcv[z_order[1]] + z_rcv[z_order[2]])
    coeffs = total.astype(BF16).astype(F32)
    pack[0:24, :] = coeffs[:, 0:128]
    pack[24:48, :] = coeffs[:, 128:256]
    pack[48:64, 0:64] = coeffs[0:16, 256:320]
    pack[48:56, 64:128] = coeffs[16:24, 256:320]
    pack[56:64, 64:128] = jnp.zeros((8, 64), F32)
    t_buf[...] = pack[...].astype(BF16)
    for d in (2, 1, 3, 0):
        zz = lax.rem(zh + d, 4)
        target = zz * 8 + y
        stays = jnp.logical_and(a == b, target == a)

        @pl.when(jnp.logical_not(stays))
        def _():
            copy(t_buf, r_ref.at[y, zl], ts.at[zz], tr.at[zl], (a, target)).start()

        @pl.when(stays)
        def _():
            pltpu.make_async_copy(t_buf, r_ref.at[y, zl], tr.at[zl]).start()

    weighted = jnp.concatenate([coeffs[:, :PANEL] * w_ref[...], jnp.zeros((8, PANEL), F32)], axis=0)
    w_buf[...] = weighted.astype(BF16)
    wo_ref[b] = weighted.astype(BF16)

    def panel(p):
        return copy(w_buf, wo_ref.at[b], ps.at[p], pr.at[b], (p, a))

    def panel_in(p):
        return copy(w_buf, wo_ref.at[p], ps.at[p], pr.at[p], (p, a))

    def over_band(fn):
        lax.fori_loop(1, NB, lambda d, carry: (fn(lax.rem(b + d, NB)), carry)[1], 0)

    over_band(lambda p: panel(p).start())
    def along_x(ee, src_x, xx, s):
        return copy(r_ref.at[ee, s], r_ref.at[ee, s], xas.at[xx, s], xar.at[src_x, s], at_x(xx))

    def along_core(ee, s):
        return copy(r_ref.at[ee, s], r_ref.at[ee, s], cas.at[ee, s], car.at[ee, s], (b, other))

    for s in range(4):
        pltpu.make_async_copy(t_buf, r_ref.at[e, s], tr.at[s]).wait()
        for xx in order[:3]:
            along_x(e, x, xx, s).start()
        along_core(e, s).start()
    for s in range(4):
        for xx in order[:3]:
            ee = xx * 2 + c
            along_x(ee, xx, xx, s).wait_recv()
            along_core(ee, s).start()
    over_band(lambda p: panel_in(p).wait_recv())
    for s in range(4):
        for xx in order:
            along_core(xx * 2 + 1 - c, s).wait_recv()
    for op in core + x_ops + z_ops:
        op.wait_send()
    for d in range(4):
        zz = lax.rem(zh + d, 4)
        target = zz * 8 + y

        @pl.when(jnp.logical_not(jnp.logical_and(a == b, target == a)))
        def _():
            copy(t_buf, r_ref.at[y, zl], ts.at[zz], tr.at[zl], (a, target)).wait_send()

    over_band(lambda p: panel(p).wait_send())
    for s in range(4):
        for xx in order[:3]:
            along_x(e, x, xx, s).wait_send()
        for xx in order:
            along_core(xx * 2 + c, s).wait_send()


def chi_kernel(r_ref, wo_ref, out_ref, left, right):
    def place(s, carry):
        ee = lax.div(s, 4)
        zl = lax.rem(s, 4)
        block = r_ref[ee, zl].astype(F32)
        row = pl.multiple_of(s * 24, 8)
        left[pl.ds(row, 24), 0:128] = block[0:24]
        left[pl.ds(row, 24), 128:256] = block[24:48]
        left[pl.ds(row, 16), 256:320] = block[48:64, 0:64]
        left[pl.ds(row + 16, 8), 256:320] = block[48:56, 64:128]
        right[pl.ds(row, 24), :] = wo_ref[zl * 8 + ee].astype(F32)[0:24]
        return carry

    lax.fori_loop(0, NB, place, 0)
    out_ref[...] = lax.dot_general(
        left[...].astype(BF16),
        right[...].astype(BF16),
        (((0,), (0,)), ((), ())),
        preferred_element_type=F32,
    )


def per_device(valence, conduction, owners, val_energy, cond_energy, gvec_index, ztab, ytab, xtab):
    dma = pltpu.SemaphoreType.DMA
    piece = (NB, 32, 128)
    fields, gvecs = pl.pallas_call(
        spread_kernel,
        out_shape=(
            jax.ShapeDtypeStruct(piece, BF16),
            jax.ShapeDtypeStruct((NGA, 1, NGD), jnp.int32),
        ),
        in_specs=[SMEM, VMEM, VMEM],
        out_specs=(VMEM, VMEM),
        scratch_shapes=[pltpu.VMEM(piece, BF16), pltpu.VMEM(piece, BF16)] + [dma((NB,))] * 6,
        compiler_params=pltpu.CompilerParams(collective_id=0, has_side_effects=True),
    )(owners, valence.reshape(piece), gvec_index.reshape(1, NGD))

    me = lax.axis_index("ga").reshape(1).astype(jnp.int32)
    partial_coeffs = pl.pallas_call(
        compute_kernel,
        out_shape=jax.ShapeDtypeStruct((2, 4, 4, 2 * NF, NGD), F32),
        in_specs=[SMEM] + [VMEM] * 6,
        out_specs=VMEM,
        scratch_shapes=[pltpu.VMEM((64 * KB, 128), F32)],
    )(me, conduction, fields.reshape(NV, 4, NGRID, NGRID), gvecs, ztab, ytab, xtab)

    weights = (1.0 / (val_energy[None, :] - cond_energy[:, None])).reshape(NF, 1)
    weights = jnp.broadcast_to(jnp.concatenate([weights, weights], axis=0), (2 * NF, PANEL))
    spread, panel = pl.pallas_call(
        exchange_kernel,
        out_shape=(
            jax.ShapeDtypeStruct((8, 4, 64, 128), BF16),
            jax.ShapeDtypeStruct((NB, 32, PANEL), BF16),
        ),
        in_specs=[VMEM, VMEM],
        out_specs=(VMEM, VMEM),
        scratch_shapes=[
            pltpu.VMEM((4, 4, 2 * NF, NGD), F32),
            pltpu.VMEM((4, 4, 2 * NF, NGD), F32),
            pltpu.VMEM((4, 4, 2 * NF, NGD), F32),
            pltpu.VMEM((4, 2 * NF, NGD), F32),
            pltpu.VMEM((4, 2 * NF, NGD), F32),
            pltpu.VMEM((64, 128), F32),
            pltpu.VMEM((64, 128), BF16),
            pltpu.VMEM((32, PANEL), BF16),
        ]
        + [dma((4,))] * 8
        + [dma((NB,))] * 2
        + [dma((4, 4))] * 2
        + [dma((8, 4))] * 2,
        compiler_params=pltpu.CompilerParams(collective_id=1, has_side_effects=True),
    )(partial_coeffs, weights)

    return pl.pallas_call(
        chi_kernel,
        out_shape=jax.ShapeDtypeStruct((NGD, PANEL), F32),
        in_specs=[VMEM, VMEM],
        out_specs=VMEM,
        scratch_shapes=[pltpu.VMEM((NB * 24, NGD), F32), pltpu.VMEM((NB * 24, PANEL), F32)],
    )(spread, panel)


def solution(mesh):
    ztab, ytab, xtab = (jnp.asarray(t) for t in tables())

    def step(valence, conduction, owners, val_energy, cond_energy, gvec_index):
        return jax.shard_map(
            per_device,
            mesh=mesh,
            in_specs=(
                P("band", None, "ga", None, None),
                P("band", "ga", None, None),
                P(),
                P(),
                P("band"),
                P("ga"),
                P(),
                P(),
                P(),
            ),
            out_specs=P("band", "ga"),
            check_vma=False,
        )(valence, conduction, owners, val_energy, cond_energy, gvec_index, ztab, ytab, xtab)

    return step
```

```python
import math

import jax
import jax.numpy as jnp
import numpy as np
from jax import lax
from jax.experimental import pallas as pl
from jax.experimental.pallas import tpu as pltpu
from jax.sharding import PartitionSpec as P

NGRID = 128
KB = 64
NV = 2
NC = 6
NF = NV * NC
NGD = 320
PANEL = 128
NB = 32
NGA = 32

F32 = jnp.float32
BF16 = jnp.bfloat16
MESH = pl.DeviceIdType.MESH
VMEM = pl.BlockSpec(memory_space=pltpu.VMEM)
SMEM = pl.BlockSpec(memory_space=pltpu.SMEM)


def split_table(table, terms):
    parts = []
    rest = table.astype(np.float32)
    for _ in range(terms):
        part = rest.astype(jnp.bfloat16)
        parts.append(part)
        rest = rest - part.astype(np.float32)
    return parts


def tables():
    n = np.arange(NGRID)[:, None]
    m = np.arange(KB)[None, :] - KB // 2
    angle = ((n * m) % NGRID).astype(np.float64) * (2.0 * math.pi / NGRID)
    scale = 1.0 / math.sqrt(NGRID)
    c = np.cos(angle) * scale
    s = -np.sin(angle) * scale
    zh, zl = split_table(np.concatenate([c, s], axis=1), 2)
    ztab = np.concatenate([np.concatenate([zh, zh], axis=0), np.concatenate([zl, zl], axis=0)], axis=1)
    yh, yl = split_table(np.concatenate([c.T, s.T], axis=0), 2)
    ytab = np.concatenate([np.concatenate([yh, yh], axis=1), np.concatenate([yl, yl], axis=1)], axis=0)
    own = np.concatenate([c.reshape(NGA, 4, KB), s.reshape(NGA, 4, KB)], axis=1)
    parts = split_table(own, 3)
    xtab = np.concatenate(parts + [np.zeros_like(parts[0])], axis=1)
    return ztab, ytab, xtab


def spread_kernel(own_ref, val_ref, gv_ref, out_ref, gva_ref, masked, recv, ss, sr, gs, gr, vs, vr):
    b = lax.axis_index("band")
    a = lax.axis_index("ga")
    barrier = pltpu.get_barrier_semaphore()

    def greet(d, carry):
        pl.semaphore_signal(barrier, 1, device_id=(lax.rem(b + d, NB), a), device_id_type=MESH)
        pl.semaphore_signal(barrier, 1, device_id=(b, lax.rem(a + d, NGA)), device_id_type=MESH)
        return carry

    lax.fori_loop(1, NB, greet, 0)
    half = NB // NV
    for k in range(NV):
        flag = jnp.where(own_ref[k] == b, 1.0, 0.0).astype(F32)
        block = val_ref[k * half : (k + 1) * half].astype(F32)
        masked[k * half : (k + 1) * half] = (block * flag).astype(BF16)
    gva_ref[a] = gv_ref[...].reshape(1, NGD)
    pl.semaphore_wait(barrier, 2 * (NB - 1))

    def piece(p):
        return pltpu.make_async_remote_copy(
            masked.at[p], recv.at[b], ss.at[p], sr.at[b], device_id=(p, a), device_id_type=MESH
        )

    def piece_in(p):
        return pltpu.make_async_remote_copy(
            masked.at[p], recv.at[p], ss.at[p], sr.at[p], device_id=(p, a), device_id_type=MESH
        )

    def whole(p):
        return pltpu.make_async_remote_copy(
            out_ref.at[b], out_ref.at[b], gs.at[p], gr.at[b], device_id=(p, a), device_id_type=MESH
        )

    def whole_in(p):
        return pltpu.make_async_remote_copy(
            out_ref.at[b], out_ref.at[p], gs.at[p], gr.at[p], device_id=(p, a), device_id_type=MESH
        )

    def gvec(q):
        return pltpu.make_async_remote_copy(
            gva_ref.at[a], gva_ref.at[a], vs.at[q], vr.at[a], device_id=(b, q), device_id_type=MESH
        )

    def gvec_in(q):
        return pltpu.make_async_remote_copy(
            gva_ref.at[a], gva_ref.at[q], vs.at[q], vr.at[q], device_id=(b, q), device_id_type=MESH
        )

    def over_band(fn):
        lax.fori_loop(1, NB, lambda d, carry: (fn(lax.rem(b + d, NB)), carry)[1], 0)

    def over_ga(fn):
        lax.fori_loop(1, NGA, lambda d, carry: (fn(lax.rem(a + d, NGA)), carry)[1], 0)

    over_band(lambda p: piece(p).start())
    over_ga(lambda q: gvec(q).start())

    def add(d, total):
        p = lax.rem(b + NB - d, NB)
        piece_in(p).wait_recv()
        return total + recv[p].astype(F32)

    total = lax.fori_loop(1, NB, add, masked[b].astype(F32))
    out_ref[b] = total.astype(BF16)
    over_band(lambda p: whole(p).start())
    over_ga(lambda q: gvec_in(q).wait_recv())
    over_band(lambda p: whole_in(p).wait_recv())
    over_band(lambda p: piece(p).wait_send())
    over_band(lambda p: whole(p).wait_send())
    over_ga(lambda q: gvec(q).wait_send())


def dot(x, y):
    return jnp.dot(x, y, preferred_element_type=F32)


def split(x):
    high = x.astype(BF16)
    return high, (x - high.astype(F32)).astype(BF16)


def dot(x, y):
    return jnp.dot(x, y, preferred_element_type=F32)


def split(x):
    high = x.astype(BF16)
    return high, (x - high.astype(F32)).astype(BF16)


def main_kernel(
    ve_ref, ce_ref, cond_ref, val_ref, gva_ref, zt_ref, yt_ref, xt_ref, out_ref,
    z_scr, y_scr, p_buf, c_rcv, s1, x_rcv, s2, z_rcv, t_buf, w_buf, r_ref, wo_ref, left, right,
    cs, cr, xs, xr, zs, zr, ts, tr, ps, pr, xas, xar, cas, car,
):
    b = lax.axis_index("band")
    a = lax.axis_index("ga")
    zl, y = lax.div(b, 8), lax.rem(b, 8)
    zh, x, c = lax.div(a, 8), lax.rem(lax.div(a, 2), 4), lax.rem(a, 2)
    e = lax.rem(a, 8)
    other = a + 1 - 2 * c
    barrier = pltpu.get_barrier_semaphore()

    def copy(src, dst, send, recv, where):
        return pltpu.make_async_remote_copy(
            src, dst, send, recv, device_id=where, device_id_type=MESH
        )

    def at_x(xx):
        return (b, zh * 8 + xx * 2 + c)

    def at_z(zz):
        return (b, zz * 8 + x * 2 + c)

    def greet(band, ga):
        pl.semaphore_signal(barrier, 1, device_id=(band, ga), device_id_type=MESH)

    for s in range(4):
        source = s * 8 + e

        @pl.when(jnp.logical_or(source != b, a != b))
        def _():
            greet(source, b)

    for d in (2, 1, 3):
        greet(*at_z(lax.rem(zh + d, 4)))
        greet(*at_x(lax.rem(x + d, 4)))
    greet(b, other)

    def greet_band(d, carry):
        greet(lax.rem(b + d, NB), a)
        return carry

    lax.fori_loop(1, NB, greet_band, 0)

    for xl in range(4):
        y_scr[(xl * 16 + NF) * KB : (xl + 1) * 16 * KB, :] = jnp.zeros((4 * KB, 128), F32)
    low = lax.broadcasted_iota(jnp.int32, (1, 128), 1) < KB
    sign = jnp.where(low, -1.0, 1.0).astype(F32)

    def along_z(f):
        pair = cond_ref[lax.div(f, NV)].astype(F32) * val_ref[lax.rem(f, NV)].astype(F32)
        hl = jnp.concatenate(split(pair.reshape(4 * NGRID, NGRID)), axis=1)
        both = dot(hl, zt_ref[...])
        high, rest = split(both[:, :128] + both[:, 128:])
        for xl in range(4):
            rows = slice(xl * NGRID, (xl + 1) * NGRID)
            z_scr[xl // 2, 0:NGRID, (xl % 2) * 128 : (xl % 2 + 1) * 128] = high[rows]
            z_scr[xl // 2, NGRID : 2 * NGRID, (xl % 2) * 128 : (xl % 2 + 1) * 128] = rest[rows]

    def along_y(f):
        for pair in range(2):
            both = dot(yt_ref[...], z_scr[pair])
            sums = both[:128] + both[128:]
            for i in range(2):
                part = sums[:, i * 128 : (i + 1) * 128]
                row = pl.multiple_of(((2 * pair + i) * 16 + f) * KB, KB)
                y_scr[pl.ds(row, KB), :] = part[:KB] + pltpu.roll(part[KB:], KB, 1) * sign

    def field(f, carry):
        along_y(f - 1)
        along_z(f)
        return carry

    along_z(0)
    lax.fori_loop(1, NF, field, 0)
    along_y(NF - 1)

    xt = xt_ref[a]
    lane = lax.broadcasted_iota(jnp.int32, (64, 128), 1) < KB
    cell = lax.broadcasted_iota(jnp.int32, (128, NGD), 0)
    xcell = lax.broadcasted_iota(jnp.int32, (KB, NGD), 0)

    def select(zz, xx, cc):
        j = zz * 8 + xx * 2 + cc
        y0 = y_scr[pl.ds(2 * j, 64, stride=KB), :]
        y1 = y_scr[pl.ds(2 * j + 1, 64, stride=KB), :]
        ur = jnp.where(lane, y0, pltpu.roll(y1, KB, 1))
        ui = jnp.where(lane, pltpu.roll(y0, KB, 1), y1)
        hl = jnp.concatenate(split(jnp.concatenate([ur, ui], axis=0)), axis=1)
        v = gva_ref[j]
        hot = jnp.where(cell == (v & 127), 1.0, 0.0).astype(BF16)
        xhot = jnp.where(xcell == (v >> 7), 1.0, 0.0).astype(BF16)
        sel = dot(hl, jnp.concatenate([hot, hot], axis=0))
        e3 = dot(xt, xhot)
        phase = e3[0:8] + (e3[8:16] + e3[16:24])
        re = jnp.zeros((16, NGD), F32)
        im = jnp.zeros((16, NGD), F32)
        for xl in range(4):
            sr = sel[xl * 16 : (xl + 1) * 16]
            si = sel[64 + xl * 16 : 64 + (xl + 1) * 16]
            er = phase[xl : xl + 1]
            ei = phase[4 + xl : 5 + xl]
            re = re + (sr * er - si * ei)
            im = im + (si * er + sr * ei)
        rows = jnp.concatenate([re[:NF], im[:NF]], axis=0)
        p_buf[cc, zz, xx, 0:24] = rows[:, 0:128]
        p_buf[cc, zz, xx, 24:48] = rows[:, 128:256]
        p_buf[cc, zz, xx, 48:64, 0:64] = rows[0:16, 256:320]
        p_buf[cc, zz, xx, 48:56, 64:128] = rows[16:24, 256:320]
        p_buf[cc, zz, xx, 56:64, 64:128] = jnp.zeros((8, 64), F32)

    def select_group(zz):
        def pair(xx, carry):
            select(zz, xx, 1 - c)
            select(zz, xx, c)
            return carry

        lax.fori_loop(0, 4, pair, 0)

    x_order = [lax.rem(x + d, 4) for d in (2, 1, 3)]
    z_order = [lax.rem(zh + d, 4) for d in (2, 1, 3)] + [zh]

    def to_core(zz):
        return copy(p_buf.at[1 - c, zz], c_rcv.at[zz], cs.at[zz], cr.at[zz], (b, other))

    def to_x(zz, xx):
        return copy(s1.at[zz, xx], x_rcv.at[x, zz], xs.at[xx, zz], xr.at[x, zz], at_x(xx))

    def from_x(zz, xx):
        return copy(s1.at[zz, xx], x_rcv.at[xx, zz], xs.at[xx, zz], xr.at[xx, zz], at_x(xx))

    def to_z(zz):
        return copy(s2.at[zz], z_rcv.at[zh], zs.at[zz], zr.at[zh], at_z(zz))

    def from_z(zz):
        return copy(s2.at[zz], z_rcv.at[zz], zs.at[zz], zr.at[zz], at_z(zz))

    def core_done(zz):
        to_core(zz).wait_recv()
        s1[zz] = p_buf[c, zz] + c_rcv[zz]
        for xx in x_order:
            to_x(zz, xx).start()

    def x_done(zz):
        for xx in x_order:
            from_x(zz, xx).wait_recv()
        s2[zz] = (s1[zz, x] + x_rcv[x_order[0], zz]) + (x_rcv[x_order[1], zz] + x_rcv[x_order[2], zz])

    for i, zz in enumerate(z_order):
        select_group(zz)
        if i == 0:
            pl.semaphore_wait(barrier, 38 + 4 - jnp.where(a == b, 1, 0))
        to_core(zz).start()
        if i:
            core_done(z_order[i - 1])
    core_done(zh)
    for zz in z_order[:3]:
        x_done(zz)
        to_z(zz).start()
    x_done(zh)
    row = lax.rem(lax.broadcasted_iota(jnp.int32, (24, PANEL), 0), NF)
    ve = jnp.where(lax.rem(row, NV) == 0, ve_ref[0], ve_ref[1])
    ce = jnp.full((24, PANEL), ce_ref[0], F32)
    for i in range(1, NC):
        ce = jnp.where(lax.div(row, NV) == i, ce_ref[i], ce)
    weights = 1.0 / (ve - ce)
    for zz in z_order[:3]:
        from_z(zz).wait_recv()
    total = (s2[zh] + z_rcv[z_order[0]]) + (z_rcv[z_order[1]] + z_rcv[z_order[2]])
    coeffs = total.astype(BF16)
    t_buf[...] = coeffs
    for zz in z_order:
        target = zz * 8 + y
        stays = jnp.logical_and(a == b, target == a)

        @pl.when(jnp.logical_not(stays))
        def _():
            copy(t_buf, r_ref.at[y, zl], ts.at[zz], tr.at[zl], (a, target)).start()

        @pl.when(stays)
        def _():
            pltpu.make_async_copy(t_buf, r_ref.at[y, zl], tr.at[zl]).start()

    weighted = coeffs.astype(F32)[0:24] * weights
    weighted = jnp.concatenate([weighted, jnp.zeros((8, PANEL), F32)], axis=0).astype(BF16)
    w_buf[...] = weighted
    wo_ref[b] = weighted

    def panel(p):
        return copy(w_buf, wo_ref.at[b], ps.at[p], pr.at[b], (p, a))

    def panel_in(p):
        return copy(w_buf, wo_ref.at[p], ps.at[p], pr.at[p], (p, a))

    def over_band(fn):
        lax.fori_loop(1, NB, lambda d, carry: (fn(lax.rem(b + d, NB)), carry)[1], 0)

    over_band(lambda p: panel(p).start())

    def along_x(ee, src_x, xx, s):
        return copy(r_ref.at[ee, s], r_ref.at[ee, s], xas.at[xx, s], xar.at[src_x, s], at_x(xx))

    def along_core(ee, s):
        return copy(r_ref.at[ee, s], r_ref.at[ee, s], cas.at[ee, s], car.at[ee, s], (b, other))

    def place(base, ee, s):
        at = (base + s) * 24
        block = r_ref[ee, s].astype(F32)
        left[at : at + 24, 0:128] = block[0:24]
        left[at : at + 24, 128:256] = block[24:48]
        left[at : at + 16, 256:320] = block[48:64, 0:64]
        left[at + 16 : at + 24, 256:320] = block[48:56, 64:128]

    def place_weighted(base, ee):
        for s in range(4):
            at = (base + s) * 24
            right[at : at + 24, :] = wo_ref[s * 8 + ee].astype(F32)[0:24]

    def product(half):
        rows = slice(half * 384, (half + 1) * 384)
        return lax.dot_general(
            left[rows].astype(BF16),
            right[rows].astype(BF16),
            (((0,), (0,)), ((), ())),
            preferred_element_type=F32,
        )

    for s in range(4):
        pltpu.make_async_copy(t_buf, r_ref.at[e, s], tr.at[s]).wait()
        for xx in x_order:
            along_x(e, x, xx, s).start()
        along_core(e, s).start()
        place(0, e, s)
    for s in range(4):
        for i, xx in enumerate(x_order):
            ee = xx * 2 + c
            along_x(ee, xx, xx, s).wait_recv()
            along_core(ee, s).start()
            place(4 + 4 * i, ee, s)
    over_band(lambda p: panel_in(p).wait_recv())
    for i, xx in enumerate([x] + x_order):
        place_weighted(4 * i, xx * 2 + c)
        place_weighted(16 + 4 * i, xx * 2 + 1 - c)
    chi = product(0)
    for i, xx in enumerate([x] + x_order):
        for s in range(4):
            along_core(xx * 2 + 1 - c, s).wait_recv()
            place(16 + 4 * i, xx * 2 + 1 - c, s)
    out_ref[...] = chi + product(1)
    for zz in z_order:
        to_core(zz).wait_send()
        for xx in x_order:
            to_x(zz, xx).wait_send()
    for zz in z_order[:3]:
        to_z(zz).wait_send()
    for zz in z_order:
        target = zz * 8 + y

        @pl.when(jnp.logical_not(jnp.logical_and(a == b, target == a)))
        def _():
            copy(t_buf, r_ref.at[y, zl], ts.at[zz], tr.at[zl], (a, target)).wait_send()

    over_band(lambda p: panel(p).wait_send())
    for s in range(4):
        for xx in x_order:
            along_x(e, x, xx, s).wait_send()
        for xx in [x] + x_order:
            along_core(xx * 2 + c, s).wait_send()


def per_device(valence, conduction, owners, val_energy, cond_energy, gvec_index, ztab, ytab, xtab):
    dma = pltpu.SemaphoreType.DMA
    piece = (NB, 32, 128)
    fields, gvecs = pl.pallas_call(
        spread_kernel,
        out_shape=(
            jax.ShapeDtypeStruct(piece, BF16),
            jax.ShapeDtypeStruct((NGA, 1, NGD), jnp.int32),
        ),
        in_specs=[SMEM, VMEM, VMEM],
        out_specs=(VMEM, VMEM),
        scratch_shapes=[pltpu.VMEM(piece, BF16), pltpu.VMEM(piece, BF16)] + [dma((NB,))] * 6,
        compiler_params=pltpu.CompilerParams(collective_id=0, has_side_effects=True),
    )(owners, valence.reshape(piece), gvec_index)

    tile = (64, 128)
    return pl.pallas_call(
        main_kernel,
        out_shape=jax.ShapeDtypeStruct((NGD, PANEL), F32),
        in_specs=[SMEM, SMEM] + [VMEM] * 6,
        out_specs=VMEM,
        scratch_shapes=[
            pltpu.VMEM((2, 2 * NGRID, 2 * NGRID), BF16),
            pltpu.VMEM((64 * KB, 128), F32),
            pltpu.VMEM((2, 4, 4) + tile, F32),
            pltpu.VMEM((4, 4) + tile, F32),
            pltpu.VMEM((4, 4) + tile, F32),
            pltpu.VMEM((4, 4) + tile, F32),
            pltpu.VMEM((4,) + tile, F32),
            pltpu.VMEM((4,) + tile, F32),
            pltpu.VMEM(tile, BF16),
            pltpu.VMEM((32, PANEL), BF16),
            pltpu.VMEM((8, 4) + tile, BF16),
            pltpu.VMEM((NB, 32, PANEL), BF16),
            pltpu.VMEM((NB * 24, NGD), F32),
            pltpu.VMEM((NB * 24, PANEL), F32),
            dma((4,)),
            dma((4,)),
            dma((4, 4)),
            dma((4, 4)),
            dma((4,)),
            dma((4,)),
            dma((4,)),
            dma((4,)),
            dma((NB,)),
            dma((NB,)),
            dma((4, 4)),
            dma((4, 4)),
            dma((8, 4)),
            dma((8, 4)),
        ],
        compiler_params=pltpu.CompilerParams(collective_id=1, has_side_effects=True),
    )(
        val_energy, cond_energy, conduction, fields.reshape(NV, 4, NGRID, NGRID), gvecs, ztab, ytab, xtab
    )


def solution(mesh):
    ztab, ytab, xtab = (jnp.asarray(t) for t in tables())

    def step(valence, conduction, owners, val_energy, cond_energy, gvec_index):
        return jax.shard_map(
            per_device,
            mesh=mesh,
            in_specs=(
                P("band", None, "ga", None, None),
                P("band", "ga", None, None),
                P(),
                P(),
                P("band"),
                P("ga"),
                P(),
                P(),
                P(),
            ),
            out_specs=P("band", "ga"),
            check_vma=False,
        )(valence, conduction, owners, val_energy, cond_energy, gvec_index, ztab, ytab, xtab)

    return step
```

```python
import math

import jax
import jax.numpy as jnp
import numpy as np
from jax import lax
from jax.experimental import pallas as pl
from jax.experimental.pallas import tpu as pltpu
from jax.sharding import PartitionSpec as P

NGRID = 128
KB = 64
NV = 2
NC = 6
NF = NV * NC
NGD = 320
PANEL = 128
NB = 32
NGA = 32

F32 = jnp.float32
BF16 = jnp.bfloat16
MESH = pl.DeviceIdType.MESH
VMEM = pl.BlockSpec(memory_space=pltpu.VMEM)
SMEM = pl.BlockSpec(memory_space=pltpu.SMEM)


def split_table(table, terms):
    parts = []
    rest = table.astype(np.float32)
    for _ in range(terms):
        part = rest.astype(jnp.bfloat16)
        parts.append(part)
        rest = rest - part.astype(np.float32)
    return parts


def tables():
    n = np.arange(NGRID)[:, None]
    m = np.arange(KB)[None, :] - KB // 2
    angle = ((n * m) % NGRID).astype(np.float64) * (2.0 * math.pi / NGRID)
    scale = 1.0 / math.sqrt(NGRID)
    c = np.cos(angle) * scale
    s = -np.sin(angle) * scale
    zh, zl = split_table(np.concatenate([c, s], axis=1), 2)
    ztab = np.concatenate([np.concatenate([zh, zh], axis=0), np.concatenate([zl, zl], axis=0)], axis=1)
    yh, yl = split_table(np.concatenate([c.T, s.T], axis=0), 2)
    ytab = np.concatenate([np.concatenate([yh, yh], axis=1), np.concatenate([yl, yl], axis=1)], axis=0)
    own = np.concatenate([c.reshape(NGA, 4, KB), s.reshape(NGA, 4, KB)], axis=1)
    parts = split_table(own, 3)
    xtab = np.concatenate(parts + [np.zeros_like(parts[0])], axis=1)
    return ztab, ytab, xtab


def dot(x, y):
    return jnp.dot(x, y, preferred_element_type=F32)


def split(x):
    high = x.astype(BF16)
    return high, (x - high.astype(F32)).astype(BF16)


def dot(x, y):
    return jnp.dot(x, y, preferred_element_type=F32)


def split(x):
    high = x.astype(BF16)
    return high, (x - high.astype(F32)).astype(BF16)


def main_kernel(
    own_ref, ve_ref, ce_ref, val_ref, gv_ref, cond_hbm, zt_ref, yt_ref, xt_ref, out_ref,
    cond_ref, masked, pieces, fields, gva, hots, phases,
    z_scr, y_scr, p_buf, c_rcv, s1, x_rcv, s2, z_rcv, t_buf, w_buf, r_ref, wo_ref, left, right,
    load, ss, sr, gs, gr, vzs, vzr, vxs, vxr, vcs, vcr,
    cs, cr, xs, xr, zs, zr, ts, tr, ps, pr, xas, xar, cas, car,
):
    b = lax.axis_index("band")
    a = lax.axis_index("ga")
    zl, y = lax.div(b, 8), lax.rem(b, 8)
    zh, x, c = lax.div(a, 8), lax.rem(lax.div(a, 2), 4), lax.rem(a, 2)
    e = lax.rem(a, 8)
    other = a + 1 - 2 * c
    barrier = pltpu.get_barrier_semaphore()

    def copy(src, dst, send, recv, where):
        return pltpu.make_async_remote_copy(
            src, dst, send, recv, device_id=where, device_id_type=MESH
        )

    def at_x(xx):
        return (b, zh * 8 + xx * 2 + c)

    def at_z(zz):
        return (b, zz * 8 + x * 2 + c)

    def greet(band, ga):
        pl.semaphore_signal(barrier, 1, device_id=(band, ga), device_id_type=MESH)

    for s in range(4):
        source = s * 8 + e

        @pl.when(jnp.logical_or(source != b, a != b))
        def _():
            greet(source, b)

    for d in (2, 1, 3):
        greet(*at_z(lax.rem(zh + d, 4)))
        greet(*at_x(lax.rem(x + d, 4)))
    greet(b, other)

    def over_band(fn):
        def step(i, carry):
            u = lax.div(i, 4)
            dy = 4 + (1 - 2 * lax.rem(u, 2)) * lax.div(u + 1, 2)
            fn(lax.rem(zl + 1 + lax.rem(i, 4), 4) * 8 + lax.rem(y + dy, 8))
            return carry

        lax.fori_loop(0, NB - 1, step, 0)

    over_band(lambda p: greet(p, a))
    fetch = pltpu.make_async_copy(cond_hbm, cond_ref, load)
    fetch.start()

    for k in range(NV):
        flag = jnp.where(own_ref[k] == b, 1.0, 0.0).astype(F32)
        masked[k] = (val_ref[k].astype(F32) * flag).astype(BF16)
        pieces[k, b] = masked[k, b]
    mine = c * 16 + x * 4 + zh
    gva[mine] = gv_ref[...].reshape(1, NGD)
    for xl in range(4):
        y_scr[(xl * 16 + NF) * KB : (xl + 1) * 16 * KB, :] = jnp.zeros((4 * KB, 128), F32)

    x_order = [lax.rem(x + d, 4) for d in (2, 1, 3)]
    z_order = [lax.rem(zh + d, 4) for d in (2, 1, 3)] + [zh]

    def piece(k, p):
        return copy(masked.at[k, p], pieces.at[k, b], ss.at[k], sr.at[k], (p, a))

    def whole(k, p):
        return copy(fields.at[k, b], fields.at[k, b], gs.at[k], gr.at[k], (p, a))

    def all_pieces(k):
        return copy(masked.at[k, pl.ds(0, NB - 1)], pieces.at[k, pl.ds(0, NB - 1)], ss.at[k], sr.at[k], (b, other))

    def all_whole(k):
        return copy(fields.at[k, pl.ds(0, NB - 1)], fields.at[k, pl.ds(0, NB - 1)], gs.at[k], gr.at[k], (b, other))

    def g_z(zz, slot):
        return copy(gva.at[mine], gva.at[c * 16 + x * 4 + slot], vzs.at[zz], vzr.at[slot], at_z(zz))

    def g_x(xx, slot):
        return copy(
            gva.at[pl.ds(c * 16 + x * 4, 4)], gva.at[pl.ds(c * 16 + slot * 4, 4)], vxs.at[xx], vxr.at[slot], at_x(xx)
        )

    def g_core(slot):
        return copy(gva.at[pl.ds(c * 16, 16)], gva.at[pl.ds(slot * 16, 16)], vcs, vcr, (b, other))

    pl.semaphore_wait(barrier, 38 + 4 - jnp.where(a == b, 1, 0))
    over_band(lambda p: piece(0, p).start())
    for zz in z_order[:3]:
        g_z(zz, zh).start()
    over_band(lambda p: piece(1, p).start())
    for k in range(NV):
        all_pieces(k).wait_recv()
        total = pieces[k, 0].astype(F32)
        for s in range(1, NB):
            total = total + pieces[k, s].astype(F32)
        fields[k, b] = total.astype(BF16)
        over_band(lambda p: whole(k, p).start())
        if k == 0:
            for zz in z_order[:3]:
                g_z(zz, zz).wait_recv()
            for xx in x_order:
                g_x(xx, x).start()
    for xx in x_order:
        g_x(xx, xx).wait_recv()
    g_core(c).start()
    all_pieces(0).wait_send()
    all_pieces(1).wait_send()

    xt = xt_ref[a]
    cell = lax.broadcasted_iota(jnp.int32, (128, NGD), 0)
    xcell = lax.broadcasted_iota(jnp.int32, (KB, NGD), 0)

    def prepare(j, carry):
        v = gva[j]
        hots[j] = jnp.where(cell == (v & 127), 1.0, 0.0).astype(BF16)
        xhot = jnp.where(xcell == (v >> 7), 1.0, 0.0).astype(BF16)
        e3 = dot(xt, xhot)
        phases[j] = e3[0:8] + (e3[8:16] + e3[16:24])
        return carry

    lax.fori_loop(c * 16, c * 16 + 16, prepare, 0)
    g_core(1 - c).wait_recv()
    lax.fori_loop((1 - c) * 16, (1 - c) * 16 + 16, prepare, 0)
    for zz in z_order[:3]:
        g_z(zz, zh).wait_send()
    for xx in x_order:
        g_x(xx, x).wait_send()
    g_core(c).wait_send()
    fetch.wait()

    low = lax.broadcasted_iota(jnp.int32, (1, 128), 1) < KB
    sign = jnp.where(low, -1.0, 1.0).astype(F32)

    def along_z(g):
        wave = cond_ref[lax.rem(g, NC)].astype(F32).reshape(4 * NGRID, NGRID)
        pair = wave * fields[lax.div(g, NC)].astype(F32).reshape(4 * NGRID, NGRID)
        hl = jnp.concatenate(split(pair), axis=1)
        both = dot(hl, zt_ref[...])
        high, rest = split(both[:, :128] + both[:, 128:])
        for xl in range(4):
            rows = slice(xl * NGRID, (xl + 1) * NGRID)
            z_scr[xl // 2, 0:NGRID, (xl % 2) * 128 : (xl % 2 + 1) * 128] = high[rows]
            z_scr[xl // 2, NGRID : 2 * NGRID, (xl % 2) * 128 : (xl % 2 + 1) * 128] = rest[rows]

    def along_y(g):
        f = lax.rem(g, NC) * NV + lax.div(g, NC)
        for pair in range(2):
            both = dot(yt_ref[...], z_scr[pair])
            sums = both[:128] + both[128:]
            for i in range(2):
                part = sums[:, i * 128 : (i + 1) * 128]
                row = pl.multiple_of(((2 * pair + i) * 16 + f) * KB, KB)
                y_scr[pl.ds(row, KB), :] = part[:KB] + pltpu.roll(part[KB:], KB, 1) * sign

    def field(f, carry):
        along_y(f - 1)
        along_z(f)
        return carry

    all_whole(0).wait_recv()
    along_z(0)
    lax.fori_loop(1, NC, field, 0)
    all_whole(1).wait_recv()
    lax.fori_loop(NC, NF, field, 0)
    along_y(NF - 1)
    all_whole(0).wait_send()
    all_whole(1).wait_send()

    lane = lax.broadcasted_iota(jnp.int32, (64, 128), 1) < KB

    def select(zz, xx, cc):
        j = zz * 8 + xx * 2 + cc
        y0 = y_scr[pl.ds(2 * j, 64, stride=KB), :]
        y1 = y_scr[pl.ds(2 * j + 1, 64, stride=KB), :]
        ur = jnp.where(lane, y0, pltpu.roll(y1, KB, 1))
        ui = jnp.where(lane, pltpu.roll(y0, KB, 1), y1)
        hl = jnp.concatenate(split(jnp.concatenate([ur, ui], axis=0)), axis=1)
        slot = cc * 16 + xx * 4 + zz
        hot = hots[slot]
        sel = dot(hl, jnp.concatenate([hot, hot], axis=0))
        phase = phases[slot]
        re = jnp.zeros((16, NGD), F32)
        im = jnp.zeros((16, NGD), F32)
        for xl in range(4):
            sr = sel[xl * 16 : (xl + 1) * 16]
            si = sel[64 + xl * 16 : 64 + (xl + 1) * 16]
            er = phase[xl : xl + 1]
            ei = phase[4 + xl : 5 + xl]
            re = re + (sr * er - si * ei)
            im = im + (si * er + sr * ei)
        rows = jnp.concatenate([re[:NF], im[:NF]], axis=0)
        p_buf[cc, zz, xx, 0:24] = rows[:, 0:128]
        p_buf[cc, zz, xx, 24:48] = rows[:, 128:256]
        p_buf[cc, zz, xx, 48:64, 0:64] = rows[0:16, 256:320]
        p_buf[cc, zz, xx, 48:56, 64:128] = rows[16:24, 256:320]
        p_buf[cc, zz, xx, 56:64, 64:128] = jnp.zeros((8, 64), F32)

    def select_group(zz):
        def pair(xx, carry):
            select(zz, xx, 1 - c)
            select(zz, xx, c)
            return carry

        lax.fori_loop(0, 4, pair, 0)

    def to_core(zz):
        return copy(p_buf.at[1 - c, zz], c_rcv.at[zz], cs.at[zz], cr.at[zz], (b, other))

    def to_x(zz, xx):
        return copy(s1.at[zz, xx], x_rcv.at[x, zz], xs.at[xx, zz], xr.at[x, zz], at_x(xx))

    def from_x(zz, xx):
        return copy(s1.at[zz, xx], x_rcv.at[xx, zz], xs.at[xx, zz], xr.at[xx, zz], at_x(xx))

    def to_z(zz):
        return copy(s2.at[zz], z_rcv.at[zh], zs.at[zz], zr.at[zh], at_z(zz))

    def from_z(zz):
        return copy(s2.at[zz], z_rcv.at[zz], zs.at[zz], zr.at[zz], at_z(zz))

    def core_done(zz):
        to_core(zz).wait_recv()
        s1[zz] = p_buf[c, zz] + c_rcv[zz]
        for xx in x_order:
            to_x(zz, xx).start()

    def x_done(zz):
        for xx in x_order:
            from_x(zz, xx).wait_recv()
        s2[zz] = (s1[zz, x] + x_rcv[x_order[0], zz]) + (x_rcv[x_order[1], zz] + x_rcv[x_order[2], zz])

    for i, zz in enumerate(z_order):
        select_group(zz)
        to_core(zz).start()
        if i:
            core_done(z_order[i - 1])
    core_done(zh)
    for zz in z_order[:3]:
        x_done(zz)
        to_z(zz).start()
    x_done(zh)
    row = lax.rem(lax.broadcasted_iota(jnp.int32, (24, PANEL), 0), NF)
    ve = jnp.where(lax.rem(row, NV) == 0, ve_ref[0], ve_ref[1])
    ce = jnp.full((24, PANEL), ce_ref[0], F32)
    for i in range(1, NC):
        ce = jnp.where(lax.div(row, NV) == i, ce_ref[i], ce)
    weights = 1.0 / (ve - ce)
    for zz in z_order[:3]:
        from_z(zz).wait_recv()
    total = (s2[zh] + z_rcv[z_order[0]]) + (z_rcv[z_order[1]] + z_rcv[z_order[2]])
    coeffs = total.astype(BF16)
    t_buf[...] = coeffs
    for zz in z_order:
        target = zz * 8 + y
        stays = jnp.logical_and(a == b, target == a)

        @pl.when(jnp.logical_not(stays))
        def _():
            copy(t_buf, r_ref.at[y, zl], ts.at[zz], tr.at[zl], (a, target)).start()

        @pl.when(stays)
        def _():
            pltpu.make_async_copy(t_buf, r_ref.at[y, zl], tr.at[zl]).start()

    weighted = coeffs.astype(F32)[0:24] * weights
    weighted = jnp.concatenate([weighted, jnp.zeros((8, PANEL), F32)], axis=0).astype(BF16)
    w_buf[...] = weighted
    wo_ref[b] = weighted

    def panel(p):
        return copy(w_buf, wo_ref.at[b], ps, pr, (p, a))

    def all_panels():
        return copy(wo_ref.at[pl.ds(0, NB - 1)], wo_ref.at[pl.ds(0, NB - 1)], ps, pr, (b, other))

    over_band(lambda p: panel(p).start())
    for zz in z_order:
        to_core(zz).wait_send()
        for xx in x_order:
            to_x(zz, xx).wait_send()
    for zz in z_order[:3]:
        to_z(zz).wait_send()

    def along_x(ee, src_x, xx, s):
        return copy(r_ref.at[ee, s], r_ref.at[ee, s], xas.at[xx, s], xar.at[src_x, s], at_x(xx))

    def along_core(ee, s):
        return copy(r_ref.at[ee, s], r_ref.at[ee, s], cas.at[ee, s], car.at[ee, s], (b, other))

    def place(base, ee, s):
        at = (base + s) * 24
        block = r_ref[ee, s].astype(F32)
        left[at : at + 24, 0:128] = block[0:24]
        left[at : at + 24, 128:256] = block[24:48]
        left[at : at + 16, 256:320] = block[48:64, 0:64]
        left[at + 16 : at + 24, 256:320] = block[48:56, 64:128]

    def place_weighted(base, ee):
        for s in range(4):
            at = (base + s) * 24
            right[at : at + 24, :] = wo_ref[s * 8 + ee].astype(F32)[0:24]

    def product(half):
        rows = slice(half * 384, (half + 1) * 384)
        return lax.dot_general(
            left[rows].astype(BF16),
            right[rows].astype(BF16),
            (((0,), (0,)), ((), ())),
            preferred_element_type=F32,
        )

    for s in range(4):
        pltpu.make_async_copy(t_buf, r_ref.at[e, s], tr.at[s]).wait()
        for xx in x_order:
            along_x(e, x, xx, s).start()
        along_core(e, s).start()
        place(0, e, s)
    for s in range(4):
        for i, xx in enumerate(x_order):
            ee = xx * 2 + c
            along_x(ee, xx, xx, s).wait_recv()
            along_core(ee, s).start()
            place(4 + 4 * i, ee, s)
    all_panels().wait_recv()
    for i, xx in enumerate([x] + x_order):
        place_weighted(4 * i, xx * 2 + c)
        place_weighted(16 + 4 * i, xx * 2 + 1 - c)
    for zz in z_order:
        target = zz * 8 + y

        @pl.when(jnp.logical_not(jnp.logical_and(a == b, target == a)))
        def _():
            copy(t_buf, r_ref.at[y, zl], ts.at[zz], tr.at[zl], (a, target)).wait_send()

    all_panels().wait_send()
    chi = product(0)
    for i, xx in enumerate([x] + x_order):
        for s in range(4):
            along_core(xx * 2 + 1 - c, s).wait_recv()
            place(16 + 4 * i, xx * 2 + 1 - c, s)
    out_ref[...] = chi + product(1)
    for s in range(4):
        for xx in x_order:
            along_x(e, x, xx, s).wait_send()
        for xx in [x] + x_order:
            along_core(xx * 2 + c, s).wait_send()


def per_device(valence, conduction, owners, val_energy, cond_energy, gvec_index, ztab, ytab, xtab):
    dma = pltpu.SemaphoreType.DMA
    piece = (NV, NB, 16, 128)
    tile = (64, 128)
    return pl.pallas_call(
        main_kernel,
        out_shape=jax.ShapeDtypeStruct((NGD, PANEL), F32),
        in_specs=[SMEM] * 3 + [VMEM] * 2 + [pl.BlockSpec(memory_space=pl.ANY)] + [VMEM] * 3,
        out_specs=VMEM,
        scratch_shapes=[
            pltpu.VMEM((NC, 4, NGRID, NGRID), BF16),
            pltpu.VMEM(piece, BF16),
            pltpu.VMEM(piece, BF16),
            pltpu.VMEM(piece, BF16),
            pltpu.VMEM((NGA, 1, NGD), jnp.int32),
            pltpu.VMEM((NGA, 128, NGD), BF16),
            pltpu.VMEM((NGA, 8, NGD), F32),
            pltpu.VMEM((2, 2 * NGRID, 2 * NGRID), BF16),
            pltpu.VMEM((64 * KB, 128), F32),
            pltpu.VMEM((2, 4, 4) + tile, F32),
            pltpu.VMEM((4, 4) + tile, F32),
            pltpu.VMEM((4, 4) + tile, F32),
            pltpu.VMEM((4, 4) + tile, F32),
            pltpu.VMEM((4,) + tile, F32),
            pltpu.VMEM((4,) + tile, F32),
            pltpu.VMEM(tile, BF16),
            pltpu.VMEM((32, PANEL), BF16),
            pltpu.VMEM((8, 4) + tile, BF16),
            pltpu.VMEM((NB, 32, PANEL), BF16),
            pltpu.VMEM((NB * 24, NGD), F32),
            pltpu.VMEM((NB * 24, PANEL), F32),
            dma,
            dma((NV,)),
            dma((NV,)),
            dma((NV,)),
            dma((NV,)),
            dma((4,)),
            dma((4,)),
            dma((4,)),
            dma((4,)),
            dma,
            dma,
            dma((4,)),
            dma((4,)),
            dma((4, 4)),
            dma((4, 4)),
            dma((4,)),
            dma((4,)),
            dma((4,)),
            dma((4,)),
            dma,
            dma,
            dma((4, 4)),
            dma((4, 4)),
            dma((8, 4)),
            dma((8, 4)),
        ],
        compiler_params=pltpu.CompilerParams(collective_id=1, has_side_effects=True),
    )(
        owners, val_energy, cond_energy, valence.reshape(piece), gvec_index, conduction, ztab, ytab, xtab
    )


def solution(mesh):
    ztab, ytab, xtab = (jnp.asarray(t) for t in tables())

    def step(valence, conduction, owners, val_energy, cond_energy, gvec_index):
        return jax.shard_map(
            per_device,
            mesh=mesh,
            in_specs=(
                P("band", None, "ga", None, None),
                P("band", "ga", None, None),
                P(),
                P(),
                P("band"),
                P("ga"),
                P(),
                P(),
                P(),
            ),
            out_specs=P("band", "ga"),
            check_vma=False,
        )(valence, conduction, owners, val_energy, cond_energy, gvec_index, ztab, ytab, xtab)

    return step
```

```python
import math

import jax
import jax.numpy as jnp
import numpy as np
from jax import lax
from jax.experimental import pallas as pl
from jax.experimental.pallas import tpu as pltpu
from jax.sharding import PartitionSpec as P

NGRID = 128
KB = 64
NV = 2
NC = 6
NF = NV * NC
NGD = 320
PANEL = 128
NB = 32
NGA = 32

F32 = jnp.float32
BF16 = jnp.bfloat16
MESH = pl.DeviceIdType.MESH
VMEM = pl.BlockSpec(memory_space=pltpu.VMEM)
SMEM = pl.BlockSpec(memory_space=pltpu.SMEM)


def split_table(table, terms):
    parts = []
    rest = table.astype(np.float32)
    for _ in range(terms):
        part = rest.astype(jnp.bfloat16)
        parts.append(part)
        rest = rest - part.astype(np.float32)
    return parts


def tables():
    n = np.arange(NGRID)[:, None]
    m = np.arange(KB)[None, :] - KB // 2
    angle = ((n * m) % NGRID).astype(np.float64) * (2.0 * math.pi / NGRID)
    scale = 1.0 / math.sqrt(NGRID)
    c = np.cos(angle) * scale
    s = -np.sin(angle) * scale
    zh, zl = split_table(np.concatenate([c, s], axis=1), 2)
    ztab = np.concatenate([np.concatenate([zh, zh], axis=0), np.concatenate([zl, zl], axis=0)], axis=1)
    yh, yl = split_table(np.concatenate([c.T, s.T], axis=0), 2)
    ytab = np.concatenate([np.concatenate([yh, yh], axis=1), np.concatenate([yl, yl], axis=1)], axis=0)
    own = np.concatenate([c.reshape(NGA, 4, KB), s.reshape(NGA, 4, KB)], axis=1)
    parts = split_table(own, 3)
    xtab = np.concatenate(parts + [np.zeros_like(parts[0])], axis=1)
    return ztab, ytab, xtab


def dot(x, y):
    return jnp.dot(x, y, preferred_element_type=F32)


def split(x):
    high = x.astype(BF16)
    return high, (x - high.astype(F32)).astype(BF16)


def dot(x, y):
    return jnp.dot(x, y, preferred_element_type=F32)


def split(x):
    high = x.astype(BF16)
    return high, (x - high.astype(F32)).astype(BF16)


def main_kernel(
    own_ref, ve_ref, ce_ref, gv_ref, val_hbm, cond_hbm, zt_hbm, yt_hbm, xt_hbm, out_ref,
    val_ref, cond_ref, zt_ref, yt_ref, xt_ref, masked, pieces, fields, gva, hots, phases,
    z_scr, y_scr, p_buf, c_rcv, s1, x_rcv, s2, z_rcv, t_buf, w_buf, r_ref, wo_ref, left, right,
    ready, load, ss, sr, gs, gr, vzs, vzr, vxs, vxr, vcs, vcr,
    cs, cr, xs, xr, zs, zr, ts, tr, ps, pr, xas, xar, cas, car,
):
    b = lax.axis_index("band")
    a = lax.axis_index("ga")
    zl, y = lax.div(b, 8), lax.rem(b, 8)
    zh, x, c = lax.div(a, 8), lax.rem(lax.div(a, 2), 4), lax.rem(a, 2)
    e = lax.rem(a, 8)
    other = a + 1 - 2 * c
    barrier = pltpu.get_barrier_semaphore()

    def copy(src, dst, send, recv, where):
        return pltpu.make_async_remote_copy(
            src, dst, send, recv, device_id=where, device_id_type=MESH
        )

    def at_x(xx):
        return (b, zh * 8 + xx * 2 + c)

    def at_z(zz):
        return (b, zz * 8 + x * 2 + c)

    def greet(band, ga):
        pl.semaphore_signal(barrier, 1, device_id=(band, ga), device_id_type=MESH)

    for d in (2, 1, 3):
        greet(*at_z(lax.rem(zh + d, 4)))
        greet(*at_x(lax.rem(x + d, 4)))
    greet(b, other)

    ys = [lax.rem(y + d, 8) for d in (4, 3, 5, 2, 6, 1, 7, 0)]

    def over_band(fn):
        def step(d, carry):
            base = lax.rem(zl + d, 4) * 8
            for yy in ys:
                fn(base + yy)
            return carry

        lax.fori_loop(1, 4, step, 0)
        for yy in ys[:7]:
            fn(zl * 8 + yy)

    over_band(lambda p: greet(p, a))
    sources = [val_hbm, cond_hbm, zt_hbm, yt_hbm, xt_hbm.at[a]]
    places = [val_ref, cond_ref, zt_ref, yt_ref, xt_ref]
    fetches = [
        pltpu.make_async_copy(source, there, load.at[i])
        for i, (source, there) in enumerate(zip(sources, places))
    ]
    for fetch in fetches:
        fetch.start()
    mine = c * 16 + x * 4 + zh
    gva[mine] = gv_ref[...].reshape(1, NGD)
    for xl in range(4):
        y_scr[(xl * 16 + NF) * KB : (xl + 1) * 16 * KB, :] = jnp.zeros((4 * KB, 128), F32)
    fetches[0].wait()

    for k in range(NV):
        flag = jnp.where(own_ref[k] == b, 1.0, 0.0).astype(F32)
        masked[k] = (val_ref[k].astype(F32) * flag).astype(BF16)
        pieces[k, b] = masked[k, b]

    x_order = [lax.rem(x + d, 4) for d in (2, 1, 3)]
    z_order = [lax.rem(zh + d, 4) for d in (2, 1, 3)] + [zh]

    def piece(k, p):
        return copy(masked.at[k, p], pieces.at[k, b], ss.at[k], sr.at[k], (p, a))

    def whole(k, p):
        return copy(fields.at[k, b], fields.at[k, b], gs.at[k], gr.at[k], (p, a))

    def all_pieces(k):
        return copy(masked.at[k, pl.ds(0, NB - 1)], pieces.at[k, pl.ds(0, NB - 1)], ss.at[k], sr.at[k], (b, other))

    def all_whole(k):
        return copy(fields.at[k, pl.ds(0, NB - 1)], fields.at[k, pl.ds(0, NB - 1)], gs.at[k], gr.at[k], (b, other))

    def g_z(zz, slot):
        return copy(gva.at[mine], gva.at[c * 16 + x * 4 + slot], vzs.at[zz], vzr.at[slot], at_z(zz))

    def g_x(xx, slot):
        return copy(
            gva.at[pl.ds(c * 16 + x * 4, 4)], gva.at[pl.ds(c * 16 + slot * 4, 4)], vxs.at[xx], vxr.at[slot], at_x(xx)
        )

    def g_core(slot):
        return copy(gva.at[pl.ds(c * 16, 16)], gva.at[pl.ds(slot * 16, 16)], vcs, vcr, (b, other))

    pl.semaphore_wait(barrier, 38)
    over_band(lambda p: piece(0, p).start())
    for zz in z_order[:3]:
        g_z(zz, zh).start()
    over_band(lambda p: piece(1, p).start())
    for k in range(NV):
        all_pieces(k).wait_recv()
        total = pieces[k, 0].astype(F32)
        for s in range(1, NB):
            total = total + pieces[k, s].astype(F32)
        fields[k, b] = total.astype(BF16)
        over_band(lambda p: whole(k, p).start())
        if k == 0:
            for zz in z_order[:3]:
                g_z(zz, zz).wait_recv()
            for xx in x_order:
                g_x(xx, x).start()
    for xx in x_order:
        g_x(xx, xx).wait_recv()
    g_core(c).start()
    all_pieces(0).wait_send()
    all_pieces(1).wait_send()

    for fetch in fetches[1:]:
        fetch.wait()
    xt = xt_ref[...]
    cell = lax.broadcasted_iota(jnp.int32, (128, NGD), 0)
    xcell = lax.broadcasted_iota(jnp.int32, (KB, NGD), 0)

    def prepare(j, carry):
        v = gva[j]
        hots[j] = jnp.where(cell == (v & 127), 1.0, 0.0).astype(BF16)
        xhot = jnp.where(xcell == (v >> 7), 1.0, 0.0).astype(BF16)
        e3 = dot(xt, xhot)
        phases[j] = e3[0:8] + (e3[8:16] + e3[16:24])
        return carry

    lax.fori_loop(c * 16, c * 16 + 16, prepare, 0)
    g_core(1 - c).wait_recv()

    @pl.when(a == b)
    def _():
        over_band(lambda p: pl.semaphore_signal(ready, 1, device_id=(p, a), device_id_type=MESH))

    lax.fori_loop((1 - c) * 16, (1 - c) * 16 + 16, prepare, 0)
    for zz in z_order[:3]:
        g_z(zz, zh).wait_send()
    for xx in x_order:
        g_x(xx, x).wait_send()
    g_core(c).wait_send()

    low = lax.broadcasted_iota(jnp.int32, (1, 128), 1) < KB
    sign = jnp.where(low, -1.0, 1.0).astype(F32)

    def along_z(g):
        wave = cond_ref[lax.rem(g, NC)].astype(F32).reshape(4 * NGRID, NGRID)
        pair = wave * fields[lax.div(g, NC)].astype(F32).reshape(4 * NGRID, NGRID)
        hl = jnp.concatenate(split(pair), axis=1)
        both = dot(hl, zt_ref[...])
        high, rest = split(both[:, :128] + both[:, 128:])
        for xl in range(4):
            rows = slice(xl * NGRID, (xl + 1) * NGRID)
            z_scr[xl // 2, 0:NGRID, (xl % 2) * 128 : (xl % 2 + 1) * 128] = high[rows]
            z_scr[xl // 2, NGRID : 2 * NGRID, (xl % 2) * 128 : (xl % 2 + 1) * 128] = rest[rows]

    def along_y(g):
        f = lax.rem(g, NC) * NV + lax.div(g, NC)
        for pair in range(2):
            both = dot(yt_ref[...], z_scr[pair])
            sums = both[:128] + both[128:]
            for i in range(2):
                part = sums[:, i * 128 : (i + 1) * 128]
                row = pl.multiple_of(((2 * pair + i) * 16 + f) * KB, KB)
                y_scr[pl.ds(row, KB), :] = part[:KB] + pltpu.roll(part[KB:], KB, 1) * sign

    def field(f, carry):
        along_y(f - 1)
        along_z(f)
        return carry

    all_whole(0).wait_recv()
    along_z(0)
    lax.fori_loop(1, NC, field, 0)
    all_whole(1).wait_recv()
    lax.fori_loop(NC, NF, field, 0)
    along_y(NF - 1)
    all_whole(0).wait_send()
    all_whole(1).wait_send()

    lane = lax.broadcasted_iota(jnp.int32, (64, 128), 1) < KB

    def select(zz, xx, cc):
        j = zz * 8 + xx * 2 + cc
        y0 = y_scr[pl.ds(2 * j, 64, stride=KB), :]
        y1 = y_scr[pl.ds(2 * j + 1, 64, stride=KB), :]
        ur = jnp.where(lane, y0, pltpu.roll(y1, KB, 1))
        ui = jnp.where(lane, pltpu.roll(y0, KB, 1), y1)
        hl = jnp.concatenate(split(jnp.concatenate([ur, ui], axis=0)), axis=1)
        slot = cc * 16 + xx * 4 + zz
        hot = hots[slot]
        sel = dot(hl, jnp.concatenate([hot, hot], axis=0))
        phase = phases[slot]
        re = jnp.zeros((16, NGD), F32)
        im = jnp.zeros((16, NGD), F32)
        for xl in range(4):
            sr = sel[xl * 16 : (xl + 1) * 16]
            si = sel[64 + xl * 16 : 64 + (xl + 1) * 16]
            er = phase[xl : xl + 1]
            ei = phase[4 + xl : 5 + xl]
            re = re + (sr * er - si * ei)
            im = im + (si * er + sr * ei)
        rows = jnp.concatenate([re[:NF], im[:NF]], axis=0)
        p_buf[cc, zz, xx, 0:24] = rows[:, 0:128]
        p_buf[cc, zz, xx, 24:48] = rows[:, 128:256]
        p_buf[cc, zz, xx, 48:64, 0:64] = rows[0:16, 256:320]
        p_buf[cc, zz, xx, 48:56, 64:128] = rows[16:24, 256:320]
        p_buf[cc, zz, xx, 56:64, 64:128] = jnp.zeros((8, 64), F32)

    def select_group(zz):
        def pair(i, carry):
            for xx in (2 * i, 2 * i + 1):
                select(zz, xx, 1 - c)
                select(zz, xx, c)
            return carry

        lax.fori_loop(0, 2, pair, 0)

    def to_core(zz):
        return copy(p_buf.at[1 - c, zz], c_rcv.at[zz], cs.at[zz], cr.at[zz], (b, other))

    def to_x(zz, xx):
        return copy(s1.at[zz, xx], x_rcv.at[x, zz], xs.at[xx, zz], xr.at[x, zz], at_x(xx))

    def from_x(zz, xx):
        return copy(s1.at[zz, xx], x_rcv.at[xx, zz], xs.at[xx, zz], xr.at[xx, zz], at_x(xx))

    def to_z(zz):
        return copy(s2.at[zz], z_rcv.at[zh], zs.at[zz], zr.at[zh], at_z(zz))

    def from_z(zz):
        return copy(s2.at[zz], z_rcv.at[zz], zs.at[zz], zr.at[zz], at_z(zz))

    def core_done(zz):
        to_core(zz).wait_recv()
        s1[zz] = p_buf[c, zz] + c_rcv[zz]
        for xx in x_order:
            to_x(zz, xx).start()

    def x_done(zz):
        for xx in x_order:
            from_x(zz, xx).wait_recv()
        s2[zz] = (s1[zz, x] + x_rcv[x_order[0], zz]) + (x_rcv[x_order[1], zz] + x_rcv[x_order[2], zz])

    for i, zz in enumerate(z_order):
        select_group(zz)
        to_core(zz).start()
        if i:
            core_done(z_order[i - 1])
    core_done(zh)
    for zz in z_order[:3]:
        x_done(zz)
        to_z(zz).start()
    x_done(zh)
    row = lax.rem(lax.broadcasted_iota(jnp.int32, (24, PANEL), 0), NF)
    ve = jnp.where(lax.rem(row, NV) == 0, ve_ref[0], ve_ref[1])
    ce = jnp.full((24, PANEL), ce_ref[0], F32)
    for i in range(1, NC):
        ce = jnp.where(lax.div(row, NV) == i, ce_ref[i], ce)
    weights = 1.0 / (ve - ce)
    for zz in z_order[:3]:
        from_z(zz).wait_recv()
    total = (s2[zh] + z_rcv[z_order[0]]) + (z_rcv[z_order[1]] + z_rcv[z_order[2]])
    coeffs = total.astype(BF16)
    t_buf[...] = coeffs
    @pl.when(a != b)
    def _():
        pl.semaphore_wait(ready, 1)

    slot = lax.rem(y + 4, 8)

    def to_rows(zz):
        return copy(t_buf, r_ref.at[slot, zl], ts.at[zz], tr.at[zl], (a, zz * 8 + slot))

    for zz in z_order:
        to_rows(zz).start()

    weighted = coeffs.astype(F32)[0:24] * weights
    weighted = jnp.concatenate([weighted, jnp.zeros((8, PANEL), F32)], axis=0).astype(BF16)
    w_buf[...] = weighted
    wo_ref[b] = weighted

    def panel(p):
        return copy(w_buf, wo_ref.at[b], ps, pr, (p, a))

    def all_panels():
        return copy(wo_ref.at[pl.ds(0, NB - 1)], wo_ref.at[pl.ds(0, NB - 1)], ps, pr, (b, other))

    over_band(lambda p: panel(p).start())
    for zz in z_order:
        to_core(zz).wait_send()
        for xx in x_order:
            to_x(zz, xx).wait_send()
    for zz in z_order[:3]:
        to_z(zz).wait_send()

    def along_x(ee, src_x, xx, s):
        return copy(r_ref.at[ee, s], r_ref.at[ee, s], xas.at[xx, s], xar.at[src_x, s], at_x(xx))

    def along_core(ee, s):
        return copy(r_ref.at[ee, s], r_ref.at[ee, s], cas.at[ee, s], car.at[ee, s], (b, other))

    def place(base, ee, s):
        at = (base + s) * 24
        block = r_ref[ee, s].astype(F32)
        left[at : at + 24, 0:128] = block[0:24]
        left[at : at + 24, 128:256] = block[24:48]
        left[at : at + 16, 256:320] = block[48:64, 0:64]
        left[at + 16 : at + 24, 256:320] = block[48:56, 64:128]

    def place_weighted(base, ee):
        for s in range(4):
            at = (base + s) * 24
            right[at : at + 24, :] = wo_ref[s * 8 + lax.rem(ee + 4, 8)].astype(F32)[0:24]

    def product(half):
        rows = slice(half * 384, (half + 1) * 384)
        return lax.dot_general(
            left[rows].astype(BF16),
            right[rows].astype(BF16),
            (((0,), (0,)), ((), ())),
            preferred_element_type=F32,
        )

    for s in range(4):
        copy(t_buf, r_ref.at[e, s], ts.at[s], tr.at[s], (b, other)).wait_recv()
        for xx in x_order:
            along_x(e, x, xx, s).start()
        along_core(e, s).start()
        place(0, e, s)
    for s in range(4):
        for i, xx in enumerate(x_order):
            ee = xx * 2 + c
            along_x(ee, xx, xx, s).wait_recv()
            along_core(ee, s).start()
            place(4 + 4 * i, ee, s)
    all_panels().wait_recv()
    for i, xx in enumerate([x] + x_order):
        place_weighted(4 * i, xx * 2 + c)
        place_weighted(16 + 4 * i, xx * 2 + 1 - c)
    for zz in z_order:
        to_rows(zz).wait_send()
    all_panels().wait_send()
    chi = product(0)
    for i, xx in enumerate([x] + x_order):
        for s in range(4):
            along_core(xx * 2 + 1 - c, s).wait_recv()
            place(16 + 4 * i, xx * 2 + 1 - c, s)
    out_ref[...] = chi + product(1)
    for s in range(4):
        for xx in x_order:
            along_x(e, x, xx, s).wait_send()
        for xx in [x] + x_order:
            along_core(xx * 2 + c, s).wait_send()


def per_device(valence, conduction, owners, val_energy, cond_energy, gvec_index, ztab, ytab, xtab):
    dma = pltpu.SemaphoreType.DMA
    piece = (NV, NB, 16, 128)
    tile = (64, 128)
    return pl.pallas_call(
        main_kernel,
        out_shape=jax.ShapeDtypeStruct((NGD, PANEL), F32),
        in_specs=[SMEM] * 3 + [VMEM] + [pl.BlockSpec(memory_space=pl.ANY)] * 5,
        out_specs=VMEM,
        scratch_shapes=[
            pltpu.VMEM(piece, BF16),
            pltpu.VMEM((NC, 4, NGRID, NGRID), BF16),
            pltpu.VMEM(ztab.shape, BF16),
            pltpu.VMEM(ytab.shape, BF16),
            pltpu.VMEM(xtab.shape[1:], BF16),
            pltpu.VMEM(piece, BF16),
            pltpu.VMEM(piece, BF16),
            pltpu.VMEM(piece, BF16),
            pltpu.VMEM((NGA, 1, NGD), jnp.int32),
            pltpu.VMEM((NGA, 128, NGD), BF16),
            pltpu.VMEM((NGA, 8, NGD), F32),
            pltpu.VMEM((2, 2 * NGRID, 2 * NGRID), BF16),
            pltpu.VMEM((64 * KB, 128), F32),
            pltpu.VMEM((2, 4, 4) + tile, F32),
            pltpu.VMEM((4, 4) + tile, F32),
            pltpu.VMEM((4, 4) + tile, F32),
            pltpu.VMEM((4, 4) + tile, F32),
            pltpu.VMEM((4,) + tile, F32),
            pltpu.VMEM((4,) + tile, F32),
            pltpu.VMEM(tile, BF16),
            pltpu.VMEM((32, PANEL), BF16),
            pltpu.VMEM((8, 4) + tile, BF16),
            pltpu.VMEM((NB, 32, PANEL), BF16),
            pltpu.VMEM((NB * 24, NGD), F32),
            pltpu.VMEM((NB * 24, PANEL), F32),
            pltpu.SemaphoreType.REGULAR,
            dma((5,)),
            dma((NV,)),
            dma((NV,)),
            dma((NV,)),
            dma((NV,)),
            dma((4,)),
            dma((4,)),
            dma((4,)),
            dma((4,)),
            dma,
            dma,
            dma((4,)),
            dma((4,)),
            dma((4, 4)),
            dma((4, 4)),
            dma((4,)),
            dma((4,)),
            dma((4,)),
            dma((4,)),
            dma,
            dma,
            dma((4, 4)),
            dma((4, 4)),
            dma((8, 4)),
            dma((8, 4)),
        ],
        compiler_params=pltpu.CompilerParams(collective_id=1, has_side_effects=True),
    )(
        owners, val_energy, cond_energy, gvec_index, valence.reshape(piece), conduction, ztab, ytab, xtab
    )


def solution(mesh):
    ztab, ytab, xtab = (jnp.asarray(t) for t in tables())

    def step(valence, conduction, owners, val_energy, cond_energy, gvec_index):
        return jax.shard_map(
            per_device,
            mesh=mesh,
            in_specs=(
                P("band", None, "ga", None, None),
                P("band", "ga", None, None),
                P(),
                P(),
                P("band"),
                P("ga"),
                P(),
                P(),
                P(),
            ),
            out_specs=P("band", "ga"),
            check_vma=False,
        )(valence, conduction, owners, val_energy, cond_energy, gvec_index, ztab, ytab, xtab)

    return step
```

```python
import math

import jax
import jax.numpy as jnp
import numpy as np
from jax import lax
from jax.experimental import pallas as pl
from jax.experimental.pallas import tpu as pltpu
from jax.sharding import PartitionSpec as P

NGRID = 128
KB = 64
NV = 2
NC = 6
NF = NV * NC
NGD = 320
PANEL = 128
NB = 32
NGA = 32

F32 = jnp.float32
BF16 = jnp.bfloat16
MESH = pl.DeviceIdType.MESH
VMEM = pl.BlockSpec(memory_space=pltpu.VMEM)
SMEM = pl.BlockSpec(memory_space=pltpu.SMEM)


def split_table(table, terms):
    parts = []
    rest = table.astype(np.float32)
    for _ in range(terms):
        part = rest.astype(jnp.bfloat16)
        parts.append(part)
        rest = rest - part.astype(np.float32)
    return parts


def tables():
    n = np.arange(NGRID)[:, None]
    m = np.arange(KB)[None, :] - KB // 2
    angle = ((n * m) % NGRID).astype(np.float64) * (2.0 * math.pi / NGRID)
    scale = 1.0 / math.sqrt(NGRID)
    c = np.cos(angle) * scale
    s = -np.sin(angle) * scale
    zh, zl = split_table(np.concatenate([c, s], axis=1), 2)
    ztab = np.concatenate([np.concatenate([zh, zh], axis=0), np.concatenate([zl, zl], axis=0)], axis=1)
    yh, yl = split_table(np.concatenate([c.T, s.T], axis=0), 2)
    ytab = np.concatenate([np.concatenate([yh, yh], axis=1), np.concatenate([yl, yl], axis=1)], axis=0)
    own = np.concatenate([c.reshape(NGA, 4, KB), s.reshape(NGA, 4, KB)], axis=1)
    parts = split_table(own, 3)
    xtab = np.concatenate(parts + [np.zeros_like(parts[0])], axis=1)
    return ztab, ytab, xtab


def dot(x, y):
    return jnp.dot(x, y, preferred_element_type=F32)


def split(x):
    high = x.astype(BF16)
    return high, (x - high.astype(F32)).astype(BF16)


def dot(x, y):
    return jnp.dot(x, y, preferred_element_type=F32)


def split(x):
    high = x.astype(BF16)
    return high, (x - high.astype(F32)).astype(BF16)


def main_kernel(
    own_hbm, ve_hbm, ce_hbm, gv_hbm, val_hbm, cond_hbm, zt_hbm, yt_hbm, xt_hbm, out_ref,
    own_ref, gv_ref, val_ref, cond_ref, ve_ref, ce_ref, zt_ref, yt_ref, xt_ref, masked, pieces, fields, gva, hots, phases,
    z_scr, y_scr, p_buf, c_rcv, s1, x_rcv, s2, z_rcv, t_buf, w_buf, r_ref, wo_ref, left, right,
    ready, load, ss, sr, gs, gr, vzs, vzr, vxs, vxr, vcs, vcr,
    cs, cr, xs, xr, zs, zr, ts, tr, ps, pr, xas, xar, cas, car,
):
    b = lax.axis_index("band")
    a = lax.axis_index("ga")
    zl, y = lax.div(b, 8), lax.rem(b, 8)
    zh, x, c = lax.div(a, 8), lax.rem(lax.div(a, 2), 4), lax.rem(a, 2)
    e = lax.rem(a, 8)
    other = a + 1 - 2 * c
    barrier = pltpu.get_barrier_semaphore()

    def copy(src, dst, send, recv, where):
        return pltpu.make_async_remote_copy(
            src, dst, send, recv, device_id=where, device_id_type=MESH
        )

    def at_x(xx):
        return (b, zh * 8 + xx * 2 + c)

    def at_z(zz):
        return (b, zz * 8 + x * 2 + c)

    def greet(band, ga):
        pl.semaphore_signal(barrier, 1, device_id=(band, ga), device_id_type=MESH)

    for d in (2, 1, 3):
        greet(*at_z(lax.rem(zh + d, 4)))
        greet(*at_x(lax.rem(x + d, 4)))
    greet(b, other)

    ys = [lax.rem(y + d, 8) for d in (4, 3, 5, 2, 6, 1, 7, 0)]

    def over_band(fn):
        def step(d, carry):
            base = lax.rem(zl + d, 4) * 8
            for yy in ys:
                fn(base + yy)
            return carry

        lax.fori_loop(1, 4, step, 0)
        for yy in ys[:7]:
            fn(zl * 8 + yy)

    over_band(lambda p: greet(p, a))
    sources = [own_hbm, gv_hbm, val_hbm, cond_hbm, ve_hbm, ce_hbm, zt_hbm, yt_hbm, xt_hbm.at[a]]
    places = [own_ref, gv_ref, val_ref, cond_ref, ve_ref, ce_ref, zt_ref, yt_ref, xt_ref]
    fetches = [
        pltpu.make_async_copy(source, there, load.at[i])
        for i, (source, there) in enumerate(zip(sources, places))
    ]
    for fetch in fetches:
        fetch.start()
    mine = c * 16 + x * 4 + zh
    fetches[1].wait()
    gva[mine] = gv_ref[...].reshape(1, NGD)
    fetches[0].wait()
    fetches[2].wait()

    for k in range(NV):
        flag = jnp.where(own_ref[k] == b, 1.0, 0.0).astype(F32)
        masked[k] = (val_ref[k].astype(F32) * flag).astype(BF16)
        pieces[k, b] = masked[k, b]

    x_order = [lax.rem(x + d, 4) for d in (2, 1, 3)]
    z_order = [lax.rem(zh + d, 4) for d in (2, 1, 3)] + [zh]

    def piece(k, p):
        return copy(masked.at[k, p], pieces.at[k, b], ss.at[k], sr.at[k], (p, a))

    def whole(k, p):
        return copy(fields.at[k, b], fields.at[k, b], gs.at[k], gr.at[k], (p, a))

    def all_pieces(k):
        return copy(masked.at[k, pl.ds(0, NB - 1)], pieces.at[k, pl.ds(0, NB - 1)], ss.at[k], sr.at[k], (b, other))

    def all_whole(k):
        return copy(fields.at[k, pl.ds(0, NB - 1)], fields.at[k, pl.ds(0, NB - 1)], gs.at[k], gr.at[k], (b, other))

    def g_z(zz, slot):
        return copy(gva.at[mine], gva.at[c * 16 + x * 4 + slot], vzs.at[zz], vzr.at[slot], at_z(zz))

    def g_x(xx, slot):
        return copy(
            gva.at[pl.ds(c * 16 + x * 4, 4)], gva.at[pl.ds(c * 16 + slot * 4, 4)], vxs.at[xx], vxr.at[slot], at_x(xx)
        )

    def g_core(slot):
        return copy(gva.at[pl.ds(c * 16, 16)], gva.at[pl.ds(slot * 16, 16)], vcs, vcr, (b, other))

    pl.semaphore_wait(barrier, 38)
    over_band(lambda p: piece(0, p).start())
    for zz in z_order[:3]:
        g_z(zz, zh).start()
    over_band(lambda p: piece(1, p).start())
    for k in range(NV):
        all_pieces(k).wait_recv()
        total = pieces[k, 0].astype(F32)
        for s in range(1, NB):
            total = total + pieces[k, s].astype(F32)
        fields[k, b] = total.astype(BF16)
        over_band(lambda p: whole(k, p).start())
        if k == 0:
            for zz in z_order[:3]:
                g_z(zz, zz).wait_recv()
            for xx in x_order:
                g_x(xx, x).start()
    for xx in x_order:
        g_x(xx, xx).wait_recv()
    g_core(c).start()
    all_pieces(0).wait_send()
    all_pieces(1).wait_send()

    for fetch in fetches[3:]:
        fetch.wait()
    xt = xt_ref[...]
    cell = lax.broadcasted_iota(jnp.int32, (128, NGD), 0)
    xcell = lax.broadcasted_iota(jnp.int32, (KB, NGD), 0)

    def prepare(j, carry):
        v = gva[j]
        hots[j] = jnp.where(cell == (v & 127), 1.0, 0.0).astype(BF16)
        xhot = jnp.where(xcell == (v >> 7), 1.0, 0.0).astype(BF16)
        e3 = dot(xt, xhot)
        e8 = e3[0:8] + (e3[8:16] + e3[16:24])
        for i in range(8):
            phases[j, i * NF : (i + 1) * NF] = jnp.broadcast_to(e8[i : i + 1], (NF, NGD))
        return carry

    lax.fori_loop(c * 16, c * 16 + 16, prepare, 0)
    g_core(1 - c).wait_recv()

    @pl.when(a == b)
    def _():
        over_band(lambda p: pl.semaphore_signal(ready, 1, device_id=(p, a), device_id_type=MESH))

    lax.fori_loop((1 - c) * 16, (1 - c) * 16 + 16, prepare, 0)
    for zz in z_order[:3]:
        g_z(zz, zh).wait_send()
    for xx in x_order:
        g_x(xx, x).wait_send()
    g_core(c).wait_send()

    low = lax.broadcasted_iota(jnp.int32, (1, 128), 1) < KB
    sign = jnp.where(low, -1.0, 1.0).astype(F32)

    def along_z(g):
        wave = cond_ref[lax.rem(g, NC)].astype(F32).reshape(4 * NGRID, NGRID)
        pair = wave * fields[lax.div(g, NC)].astype(F32).reshape(4 * NGRID, NGRID)
        hl = jnp.concatenate(split(pair), axis=1)
        both = dot(hl, zt_ref[...])
        high, rest = split(both[:, :128] + both[:, 128:])
        for xl in range(4):
            rows = slice(xl * NGRID, (xl + 1) * NGRID)
            z_scr[xl // 2, 0:NGRID, (xl % 2) * 128 : (xl % 2 + 1) * 128] = high[rows]
            z_scr[xl // 2, NGRID : 2 * NGRID, (xl % 2) * 128 : (xl % 2 + 1) * 128] = rest[rows]

    def along_y(g):
        f = lax.rem(g, NC) * NV + lax.div(g, NC)
        for pair in range(2):
            both = dot(yt_ref[...], z_scr[pair])
            sums = both[:128] + both[128:]
            for i in range(2):
                part = sums[:, i * 128 : (i + 1) * 128]
                row = pl.multiple_of(((2 * pair + i) * NF + f) * KB, KB)
                y_scr[pl.ds(row, KB), :] = part[:KB] + pltpu.roll(part[KB:], KB, 1) * sign

    def field(f, carry):
        along_y(f - 1)
        along_z(f)
        return carry

    all_whole(0).wait_recv()
    along_z(0)
    lax.fori_loop(1, NC, field, 0)
    all_whole(1).wait_recv()
    lax.fori_loop(NC, NF, field, 0)
    along_y(NF - 1)
    all_whole(0).wait_send()
    all_whole(1).wait_send()

    lane = lax.broadcasted_iota(jnp.int32, (4 * NF, 128), 1) < KB

    def select(zz, xx, cc):
        j = zz * 8 + xx * 2 + cc
        y0 = y_scr[pl.ds(2 * j, 4 * NF, stride=KB), :]
        y1 = y_scr[pl.ds(2 * j + 1, 4 * NF, stride=KB), :]
        ur = jnp.where(lane, y0, pltpu.roll(y1, KB, 1))
        ui = jnp.where(lane, pltpu.roll(y0, KB, 1), y1)
        hl = jnp.concatenate(split(jnp.concatenate([ur, ui], axis=0)), axis=1)
        slot = cc * 16 + xx * 4 + zz
        hot = hots[slot]
        sel = dot(hl, jnp.concatenate([hot, hot], axis=0))
        sr, si = sel[: 4 * NF], sel[4 * NF :]
        er, ei = phases[slot, : 4 * NF], phases[slot, 4 * NF :]
        re = sr * er - si * ei
        im = si * er + sr * ei
        re = re[: 2 * NF] + re[2 * NF :]
        im = im[: 2 * NF] + im[2 * NF :]
        re = re[:NF] + re[NF:]
        im = im[:NF] + im[NF:]
        rows = jnp.concatenate([re, im], axis=0)
        p_buf[cc, zz, xx, 0:24] = rows[:, 0:128]
        p_buf[cc, zz, xx, 24:48] = rows[:, 128:256]
        p_buf[cc, zz, xx, 48:64, 0:64] = rows[0:16, 256:320]
        p_buf[cc, zz, xx, 48:56, 64:128] = rows[16:24, 256:320]
        p_buf[cc, zz, xx, 56:64, 64:128] = jnp.zeros((8, 64), F32)

    def select_group(zz):
        def pair(i, carry):
            for xx in (2 * i, 2 * i + 1):
                select(zz, xx, 1 - c)
                select(zz, xx, c)
            return carry

        lax.fori_loop(0, 2, pair, 0)

    def to_core(zz):
        return copy(p_buf.at[1 - c, zz], c_rcv.at[zz], cs.at[zz], cr.at[zz], (b, other))

    def to_x(zz, xx):
        return copy(s1.at[zz, xx], x_rcv.at[x, zz], xs.at[xx, zz], xr.at[x, zz], at_x(xx))

    def from_x(zz, xx):
        return copy(s1.at[zz, xx], x_rcv.at[xx, zz], xs.at[xx, zz], xr.at[xx, zz], at_x(xx))

    def to_z(zz):
        return copy(s2.at[zz], z_rcv.at[zh], zs.at[zz], zr.at[zh], at_z(zz))

    def from_z(zz):
        return copy(s2.at[zz], z_rcv.at[zz], zs.at[zz], zr.at[zz], at_z(zz))

    def core_done(zz):
        to_core(zz).wait_recv()
        s1[zz] = p_buf[c, zz] + c_rcv[zz]
        for xx in x_order:
            to_x(zz, xx).start()

    def x_done(zz):
        for xx in x_order:
            from_x(zz, xx).wait_recv()
        s2[zz] = (s1[zz, x] + x_rcv[x_order[0], zz]) + (x_rcv[x_order[1], zz] + x_rcv[x_order[2], zz])

    for i, zz in enumerate(z_order):
        select_group(zz)
        to_core(zz).start()
        if i:
            core_done(z_order[i - 1])
    core_done(zh)
    for zz in z_order[:3]:
        x_done(zz)
        to_z(zz).start()
    x_done(zh)
    row = lax.rem(lax.broadcasted_iota(jnp.int32, (24, PANEL), 0), NF)
    ve = jnp.where(lax.rem(row, NV) == 0, ve_ref[0], ve_ref[1])
    ce = jnp.full((24, PANEL), ce_ref[0], F32)
    for i in range(1, NC):
        ce = jnp.where(lax.div(row, NV) == i, ce_ref[i], ce)
    weights = 1.0 / (ve - ce)
    for zz in z_order[:3]:
        from_z(zz).wait_recv()
    total = (s2[zh] + z_rcv[z_order[0]]) + (z_rcv[z_order[1]] + z_rcv[z_order[2]])
    coeffs = total.astype(BF16)
    t_buf[...] = coeffs
    @pl.when(a != b)
    def _():
        pl.semaphore_wait(ready, 1)

    slot = lax.rem(y + 4, 8)

    def to_rows(zz):
        return copy(t_buf, r_ref.at[slot, zl], ts.at[zz], tr.at[zl], (a, zz * 8 + slot))

    for zz in z_order:
        to_rows(zz).start()

    weighted = coeffs.astype(F32)[0:24] * weights
    weighted = jnp.concatenate([weighted, jnp.zeros((8, PANEL), F32)], axis=0).astype(BF16)
    w_buf[...] = weighted
    wo_ref[b] = weighted

    def panel(p):
        return copy(w_buf, wo_ref.at[b], ps, pr, (p, a))

    def all_panels():
        return copy(wo_ref.at[pl.ds(0, NB - 1)], wo_ref.at[pl.ds(0, NB - 1)], ps, pr, (b, other))

    over_band(lambda p: panel(p).start())
    for zz in z_order:
        to_core(zz).wait_send()
        for xx in x_order:
            to_x(zz, xx).wait_send()
    for zz in z_order[:3]:
        to_z(zz).wait_send()

    def along_x(ee, src_x, xx, s):
        return copy(r_ref.at[ee, s], r_ref.at[ee, s], xas.at[xx, s], xar.at[src_x, s], at_x(xx))

    def along_core(ee, s):
        return copy(r_ref.at[ee, s], r_ref.at[ee, s], cas.at[ee, s], car.at[ee, s], (b, other))

    def place(base, ee, s):
        at = (base + s) * 24
        block = r_ref[ee, s].astype(F32)
        left[at : at + 24, 0:128] = block[0:24]
        left[at : at + 24, 128:256] = block[24:48]
        left[at : at + 16, 256:320] = block[48:64, 0:64]
        left[at + 16 : at + 24, 256:320] = block[48:56, 64:128]

    def place_weighted(base, ee):
        for s in range(4):
            at = (base + s) * 24
            right[at : at + 24, :] = wo_ref[s * 8 + lax.rem(ee + 4, 8)].astype(F32)[0:24]

    def product(half):
        rows = slice(half * 384, (half + 1) * 384)
        return lax.dot_general(
            left[rows].astype(BF16),
            right[rows].astype(BF16),
            (((0,), (0,)), ((), ())),
            preferred_element_type=F32,
        )

    for s in range(4):
        copy(t_buf, r_ref.at[e, s], ts.at[s], tr.at[s], (b, other)).wait_recv()
        for xx in x_order:
            along_x(e, x, xx, s).start()
        along_core(e, s).start()
        place(0, e, s)
    for s in range(4):
        for i, xx in enumerate(x_order):
            ee = xx * 2 + c
            along_x(ee, xx, xx, s).wait_recv()
            along_core(ee, s).start()
            place(4 + 4 * i, ee, s)
    all_panels().wait_recv()
    for i, xx in enumerate([x] + x_order):
        place_weighted(4 * i, xx * 2 + c)
        place_weighted(16 + 4 * i, xx * 2 + 1 - c)
    for zz in z_order:
        to_rows(zz).wait_send()
    all_panels().wait_send()
    chi = product(0)
    for i, xx in enumerate([x] + x_order):
        for s in range(4):
            along_core(xx * 2 + 1 - c, s).wait_recv()
            place(16 + 4 * i, xx * 2 + 1 - c, s)
    out_ref[...] = chi + product(1)
    for s in range(4):
        for xx in x_order:
            along_x(e, x, xx, s).wait_send()
        for xx in [x] + x_order:
            along_core(xx * 2 + c, s).wait_send()


def per_device(valence, conduction, owners, val_energy, cond_energy, gvec_index, ztab, ytab, xtab):
    dma = pltpu.SemaphoreType.DMA
    piece = (NV, NB, 16, 128)
    tile = (64, 128)
    return pl.pallas_call(
        main_kernel,
        out_shape=pltpu.VMEM((NGD, PANEL), F32),
        in_specs=[pl.BlockSpec(memory_space=pl.ANY)] * 9,
        out_specs=VMEM,
        scratch_shapes=[
            pltpu.SMEM((NV,), jnp.int32),
            pltpu.VMEM((NGD,), jnp.int32),
            pltpu.VMEM(piece, BF16),
            pltpu.VMEM((NC, 4, NGRID, NGRID), BF16),
            pltpu.SMEM((NV,), F32),
            pltpu.SMEM((NC,), F32),
            pltpu.VMEM(ztab.shape, BF16),
            pltpu.VMEM(ytab.shape, BF16),
            pltpu.VMEM(xtab.shape[1:], BF16),
            pltpu.VMEM(piece, BF16),
            pltpu.VMEM(piece, BF16),
            pltpu.VMEM(piece, BF16),
            pltpu.VMEM((NGA, 1, NGD), jnp.int32),
            pltpu.VMEM((NGA, 128, NGD), BF16),
            pltpu.VMEM((NGA, 8 * NF, NGD), F32),
            pltpu.VMEM((2, 2 * NGRID, 2 * NGRID), BF16),
            pltpu.VMEM((4 * NF * KB, 128), F32),
            pltpu.VMEM((2, 4, 4) + tile, F32),
            pltpu.VMEM((4, 4) + tile, F32),
            pltpu.VMEM((4, 4) + tile, F32),
            pltpu.VMEM((4, 4) + tile, F32),
            pltpu.VMEM((4,) + tile, F32),
            pltpu.VMEM((4,) + tile, F32),
            pltpu.VMEM(tile, BF16),
            pltpu.VMEM((32, PANEL), BF16),
            pltpu.VMEM((8, 4) + tile, BF16),
            pltpu.VMEM((NB, 32, PANEL), BF16),
            pltpu.VMEM((NB * 24, NGD), F32),
            pltpu.VMEM((NB * 24, PANEL), F32),
            pltpu.SemaphoreType.REGULAR,
            dma((9,)),
            dma((NV,)),
            dma((NV,)),
            dma((NV,)),
            dma((NV,)),
            dma((4,)),
            dma((4,)),
            dma((4,)),
            dma((4,)),
            dma,
            dma,
            dma((4,)),
            dma((4,)),
            dma((4, 4)),
            dma((4, 4)),
            dma((4,)),
            dma((4,)),
            dma((4,)),
            dma((4,)),
            dma,
            dma,
            dma((4, 4)),
            dma((4, 4)),
            dma((8, 4)),
            dma((8, 4)),
        ],
        compiler_params=pltpu.CompilerParams(collective_id=1, has_side_effects=True),
    )(
        owners, val_energy, cond_energy, gvec_index, valence.reshape(piece), conduction, ztab, ytab, xtab
    )


def solution(mesh):
    ztab, ytab, xtab = (jnp.asarray(t) for t in tables())

    def step(valence, conduction, owners, val_energy, cond_energy, gvec_index):
        return jax.shard_map(
            per_device,
            mesh=mesh,
            in_specs=(
                P("band", None, "ga", None, None),
                P("band", "ga", None, None),
                P(),
                P(),
                P("band"),
                P("ga"),
                P(),
                P(),
                P(),
            ),
            out_specs=P("band", "ga"),
            check_vma=False,
        )(valence, conduction, owners, val_energy, cond_energy, gvec_index, ztab, ytab, xtab)

    return step
```

```python
import math

import jax
import jax.numpy as jnp
import numpy as np
from jax import lax
from jax.experimental import pallas as pl
from jax.experimental.pallas import tpu as pltpu
from jax.sharding import PartitionSpec as P

NGRID = 128
KB = 64
NV = 2
NC = 6
NF = NV * NC
NGD = 320
PANEL = 128
NB = 32
NGA = 32

F32 = jnp.float32
BF16 = jnp.bfloat16
MESH = pl.DeviceIdType.MESH
VMEM = pl.BlockSpec(memory_space=pltpu.VMEM)
SMEM = pl.BlockSpec(memory_space=pltpu.SMEM)


def split_table(table, terms):
    parts = []
    rest = table.astype(np.float32)
    for _ in range(terms):
        part = rest.astype(jnp.bfloat16)
        parts.append(part)
        rest = rest - part.astype(np.float32)
    return parts


def tables():
    n = np.arange(NGRID)[:, None]
    m = np.arange(KB)[None, :] - KB // 2
    angle = ((n * m) % NGRID).astype(np.float64) * (2.0 * math.pi / NGRID)
    scale = 1.0 / math.sqrt(NGRID)
    c = np.cos(angle) * scale
    s = -np.sin(angle) * scale
    zh, zl = split_table(np.concatenate([c, s], axis=1), 2)
    ztab = np.concatenate([np.concatenate([zh, zh], axis=0), np.concatenate([zl, zl], axis=0)], axis=1)
    yh, yl = split_table(np.concatenate([c.T, s.T], axis=0), 2)
    ytab = np.concatenate([np.concatenate([yh, yh], axis=1), np.concatenate([yl, yl], axis=1)], axis=0)
    own = np.concatenate([c.reshape(NGA, 4, KB), s.reshape(NGA, 4, KB)], axis=1)
    parts = split_table(own, 3)
    xtab = np.concatenate(parts + [np.zeros_like(parts[0])], axis=1)
    return ztab, ytab, xtab


def dot(x, y):
    return jnp.dot(x, y, preferred_element_type=F32)


def split(x):
    high = x.astype(BF16)
    return high, (x - high.astype(F32)).astype(BF16)


def dot(x, y):
    return jnp.dot(x, y, preferred_element_type=F32)


def split(x):
    high = x.astype(BF16)
    return high, (x - high.astype(F32)).astype(BF16)


def main_kernel(
    own_hbm, ve_hbm, ce_hbm, gv_hbm, val_hbm, cond_hbm, zt_hbm, yt_hbm, xt_hbm, out_ref,
    own_ref, gv_ref, val_ref, cond_ref, ve_ref, ce_ref, zt_ref, yt_ref, xt_ref, masked, pieces, fields, gva, hots, phases,
    z_scr, y_scr, p_buf, c_rcv, s1, x_rcv, s2, z_rcv, t_buf, w_buf, r_ref, wo_ref, left, right,
    ready, load, ss, sr, gs, gr, vzs, vzr, vxs, vxr, vcs, vcr,
    cs, cr, xs, xr, zs, zr, ts, tr, ps, pr, xas, xar, cas, car,
):
    b = lax.axis_index("band")
    a = lax.axis_index("ga")
    zl, y = lax.div(b, 8), lax.rem(b, 8)
    zh, x, c = lax.div(a, 8), lax.rem(lax.div(a, 2), 4), lax.rem(a, 2)
    e = lax.rem(a, 8)
    other = a + 1 - 2 * c
    barrier = pltpu.get_barrier_semaphore()

    def copy(src, dst, send, recv, where):
        return pltpu.make_async_remote_copy(
            src, dst, send, recv, device_id=where, device_id_type=MESH
        )

    def at_x(xx):
        return (b, zh * 8 + xx * 2 + c)

    def at_z(zz):
        return (b, zz * 8 + x * 2 + c)

    def greet(band, ga):
        pl.semaphore_signal(barrier, 1, device_id=(band, ga), device_id_type=MESH)

    for d in (2, 1, 3):
        greet(*at_z(lax.rem(zh + d, 4)))
        greet(*at_x(lax.rem(x + d, 4)))
    greet(b, other)

    ys = [lax.rem(y + d, 8) for d in (4, 3, 5, 2, 6, 1, 7, 0)]

    def over_band(fn):
        def step(d, carry):
            base = lax.rem(zl + d, 4) * 8
            for yy in ys:
                fn(base + yy)
            return carry

        lax.fori_loop(1, 4, step, 0)
        for yy in ys[:7]:
            fn(zl * 8 + yy)

    over_band(lambda p: greet(p, a))
    sources = [own_hbm, gv_hbm, val_hbm, cond_hbm, ve_hbm, ce_hbm, zt_hbm, yt_hbm, xt_hbm.at[a]]
    places = [own_ref, gv_ref, val_ref, cond_ref, ve_ref, ce_ref, zt_ref, yt_ref, xt_ref]
    fetches = [
        pltpu.make_async_copy(source, there, load.at[i])
        for i, (source, there) in enumerate(zip(sources, places))
    ]
    for fetch in fetches:
        fetch.start()
    mine = c * 16 + x * 4 + zh
    fetches[1].wait()
    gva[mine] = gv_ref[...].reshape(1, NGD)
    fetches[0].wait()
    fetches[2].wait()

    for k in range(NV):
        flag = jnp.where(own_ref[k] == b, 1.0, 0.0).astype(F32)
        masked[k] = (val_ref[k].astype(F32) * flag).astype(BF16)
        pieces[k, b] = masked[k, b]

    x_order = [lax.rem(x + d, 4) for d in (2, 1, 3)]
    z_order = [lax.rem(zh + d, 4) for d in (2, 1, 3)] + [zh]

    def piece(k, p):
        return copy(masked.at[k, p], pieces.at[k, b], ss.at[k], sr.at[k], (p, a))

    def whole(k, p):
        return copy(fields.at[k, b], fields.at[k, b], gs.at[k], gr.at[k], (p, a))

    def all_pieces(k):
        return copy(masked.at[k, pl.ds(0, NB - 1)], pieces.at[k, pl.ds(0, NB - 1)], ss.at[k], sr.at[k], (b, other))

    def all_whole(k):
        return copy(fields.at[k, pl.ds(0, NB - 1)], fields.at[k, pl.ds(0, NB - 1)], gs.at[k], gr.at[k], (b, other))

    def g_z(zz, slot):
        return copy(gva.at[mine], gva.at[c * 16 + x * 4 + slot], vzs.at[zz], vzr.at[slot], at_z(zz))

    def g_x(xx, slot):
        return copy(
            gva.at[pl.ds(c * 16 + x * 4, 4)], gva.at[pl.ds(c * 16 + slot * 4, 4)], vxs.at[xx], vxr.at[slot], at_x(xx)
        )

    def g_core(slot):
        return copy(gva.at[pl.ds(c * 16, 16)], gva.at[pl.ds(slot * 16, 16)], vcs, vcr, (b, other))

    pl.semaphore_wait(barrier, 38)
    over_band(lambda p: piece(0, p).start())
    for zz in z_order[:3]:
        g_z(zz, zh).start()
    over_band(lambda p: piece(1, p).start())
    for k in range(NV):
        all_pieces(k).wait_recv()
        total = pieces[k, 0].astype(F32)
        for s in range(1, NB):
            total = total + pieces[k, s].astype(F32)
        fields[k, b] = total.astype(BF16)
        over_band(lambda p: whole(k, p).start())
        if k == 0:
            for zz in z_order[:3]:
                g_z(zz, zz).wait_recv()
            for xx in x_order:
                g_x(xx, x).start()
    for xx in x_order:
        g_x(xx, xx).wait_recv()
    g_core(c).start()
    all_pieces(0).wait_send()
    all_pieces(1).wait_send()

    for fetch in fetches[3:]:
        fetch.wait()
    xt = xt_ref[...]
    cell = lax.broadcasted_iota(jnp.int32, (128, NGD), 0)
    xcell = lax.broadcasted_iota(jnp.int32, (KB, NGD), 0)

    def prepare(j, carry):
        v = gva[j]
        hots[j] = jnp.where(cell == (v & 127), 1.0, 0.0).astype(BF16)
        xhot = jnp.where(xcell == (v >> 7), 1.0, 0.0).astype(BF16)
        e3 = dot(xt, xhot)
        e8 = e3[0:8] + (e3[8:16] + e3[16:24])
        for i in range(8):
            phases[j, i * NF : (i + 1) * NF] = jnp.broadcast_to(e8[i : i + 1], (NF, NGD))
        return carry

    lax.fori_loop(c * 16, c * 16 + 16, prepare, 0)
    g_core(1 - c).wait_recv()

    @pl.when(a == b)
    def _():
        over_band(lambda p: pl.semaphore_signal(ready, 1, device_id=(p, a), device_id_type=MESH))

    lax.fori_loop((1 - c) * 16, (1 - c) * 16 + 16, prepare, 0)
    for zz in z_order[:3]:
        g_z(zz, zh).wait_send()
    for xx in x_order:
        g_x(xx, x).wait_send()
    g_core(c).wait_send()

    low = lax.broadcasted_iota(jnp.int32, (1, 128), 1) < KB
    sign = jnp.where(low, -1.0, 1.0).astype(F32)

    def along_z(g, slot):
        wave = cond_ref[lax.rem(g, NC)].astype(F32).reshape(4 * NGRID, NGRID)
        pair = wave * fields[lax.div(g, NC)].astype(F32).reshape(4 * NGRID, NGRID)
        hl = jnp.concatenate(split(pair), axis=1)
        both = dot(hl, zt_ref[...])
        high, rest = split(both[:, :128] + both[:, 128:])
        for xl in range(4):
            rows = slice(xl * NGRID, (xl + 1) * NGRID)
            z_scr[slot, xl // 2, 0:NGRID, (xl % 2) * 128 : (xl % 2 + 1) * 128] = high[rows]
            z_scr[slot, xl // 2, NGRID : 2 * NGRID, (xl % 2) * 128 : (xl % 2 + 1) * 128] = rest[rows]

    def along_y(g, slot):
        f = lax.rem(g, NC) * NV + lax.div(g, NC)
        for pair in range(2):
            both = dot(yt_ref[...], z_scr[slot, pair])
            sums = both[:128] + both[128:]
            for i in range(2):
                part = sums[:, i * 128 : (i + 1) * 128]
                row = pl.multiple_of(((2 * pair + i) * NF + f) * KB, KB)
                y_scr[pl.ds(row, KB), :] = part[:KB] + pltpu.roll(part[KB:], KB, 1) * sign

    def two_fields(i, g, first):
        along_y(g - 1, 1 - first)
        along_z(g, first)
        along_y(g, first)
        along_z(g + 1, 1 - first)
        return i

    all_whole(0).wait_recv()
    along_z(0, 0)
    lax.fori_loop(0, NC // 2 - 1, lambda i, n: two_fields(n, 2 * i + 1, 1), 0)
    along_y(NC - 2, 0)
    along_z(NC - 1, 1)
    all_whole(1).wait_recv()
    lax.fori_loop(NC // 2, NC, lambda i, n: two_fields(n, 2 * i, 0), 0)
    along_y(NF - 1, 1)
    all_whole(0).wait_send()
    all_whole(1).wait_send()

    lane = lax.broadcasted_iota(jnp.int32, (4 * NF, 128), 1) < KB

    def select(zz, xx, cc):
        j = zz * 8 + xx * 2 + cc
        y0 = y_scr[pl.ds(2 * j, 4 * NF, stride=KB), :]
        y1 = y_scr[pl.ds(2 * j + 1, 4 * NF, stride=KB), :]
        ur = jnp.where(lane, y0, pltpu.roll(y1, KB, 1))
        ui = jnp.where(lane, pltpu.roll(y0, KB, 1), y1)
        hl = jnp.concatenate(split(jnp.concatenate([ur, ui], axis=0)), axis=1)
        slot = cc * 16 + xx * 4 + zz
        hot = hots[slot]
        sel = dot(hl, jnp.concatenate([hot, hot], axis=0))
        sr, si = sel[: 4 * NF], sel[4 * NF :]
        er, ei = phases[slot, : 4 * NF], phases[slot, 4 * NF :]
        re = sr * er - si * ei
        im = si * er + sr * ei
        re = re[: 2 * NF] + re[2 * NF :]
        im = im[: 2 * NF] + im[2 * NF :]
        re = re[:NF] + re[NF:]
        im = im[:NF] + im[NF:]
        rows = jnp.concatenate([re, im], axis=0)
        p_buf[cc, zz, xx, 0:24] = rows[:, 0:128]
        p_buf[cc, zz, xx, 24:48] = rows[:, 128:256]
        p_buf[cc, zz, xx, 48:64, 0:64] = rows[0:16, 256:320]
        p_buf[cc, zz, xx, 48:56, 64:128] = rows[16:24, 256:320]
        p_buf[cc, zz, xx, 56:64, 64:128] = jnp.zeros((8, 64), F32)

    def select_group(zz):
        def pair(i, carry):
            for xx in (2 * i, 2 * i + 1):
                select(zz, xx, 1 - c)
                select(zz, xx, c)
            return carry

        lax.fori_loop(0, 2, pair, 0)

    def to_core(zz):
        return copy(p_buf.at[1 - c, zz], c_rcv.at[zz], cs.at[zz], cr.at[zz], (b, other))

    def to_x(zz, xx):
        return copy(s1.at[zz, xx], x_rcv.at[x, zz], xs.at[xx, zz], xr.at[x, zz], at_x(xx))

    def from_x(zz, xx):
        return copy(s1.at[zz, xx], x_rcv.at[xx, zz], xs.at[xx, zz], xr.at[xx, zz], at_x(xx))

    def to_z(zz):
        return copy(s2.at[zz], z_rcv.at[zh], zs.at[zz], zr.at[zh], at_z(zz))

    def from_z(zz):
        return copy(s2.at[zz], z_rcv.at[zz], zs.at[zz], zr.at[zz], at_z(zz))

    def core_done(zz):
        to_core(zz).wait_recv()
        s1[zz] = p_buf[c, zz] + c_rcv[zz]
        for xx in x_order:
            to_x(zz, xx).start()

    def x_done(zz):
        for xx in x_order:
            from_x(zz, xx).wait_recv()
        s2[zz] = (s1[zz, x] + x_rcv[x_order[0], zz]) + (x_rcv[x_order[1], zz] + x_rcv[x_order[2], zz])

    for i, zz in enumerate(z_order):
        select_group(zz)
        to_core(zz).start()
        if i:
            core_done(z_order[i - 1])
    core_done(zh)
    for zz in z_order[:3]:
        x_done(zz)
        to_z(zz).start()
    x_done(zh)
    row = lax.rem(lax.broadcasted_iota(jnp.int32, (24, PANEL), 0), NF)
    ve = jnp.where(lax.rem(row, NV) == 0, ve_ref[0], ve_ref[1])
    ce = jnp.full((24, PANEL), ce_ref[0], F32)
    for i in range(1, NC):
        ce = jnp.where(lax.div(row, NV) == i, ce_ref[i], ce)
    weights = 1.0 / (ve - ce)
    for zz in z_order[:3]:
        from_z(zz).wait_recv()
    total = (s2[zh] + z_rcv[z_order[0]]) + (z_rcv[z_order[1]] + z_rcv[z_order[2]])
    coeffs = total.astype(BF16)
    t_buf[...] = coeffs
    @pl.when(a != b)
    def _():
        pl.semaphore_wait(ready, 1)

    slot = lax.rem(y + 4, 8)

    def to_rows(zz):
        return copy(t_buf, r_ref.at[slot, zl], ts.at[zz], tr.at[zl], (a, zz * 8 + slot))

    for zz in z_order:
        to_rows(zz).start()

    weighted = coeffs.astype(F32)[0:24] * weights
    weighted = jnp.concatenate([weighted, jnp.zeros((8, PANEL), F32)], axis=0).astype(BF16)
    w_buf[...] = weighted
    wo_ref[b] = weighted

    def panel(p):
        return copy(w_buf, wo_ref.at[b], ps, pr, (p, a))

    def all_panels():
        return copy(wo_ref.at[pl.ds(0, NB - 1)], wo_ref.at[pl.ds(0, NB - 1)], ps, pr, (b, other))

    over_band(lambda p: panel(p).start())
    for zz in z_order:
        to_core(zz).wait_send()
        for xx in x_order:
            to_x(zz, xx).wait_send()
    for zz in z_order[:3]:
        to_z(zz).wait_send()

    def along_x(ee, src_x, xx, s):
        return copy(r_ref.at[ee, s], r_ref.at[ee, s], xas.at[xx, s], xar.at[src_x, s], at_x(xx))

    def along_core(ee, s):
        return copy(r_ref.at[ee, s], r_ref.at[ee, s], cas.at[ee, s], car.at[ee, s], (b, other))

    def place(base, ee, s):
        at = (base + s) * 24
        block = r_ref[ee, s].astype(F32)
        left[at : at + 24, 0:128] = block[0:24]
        left[at : at + 24, 128:256] = block[24:48]
        left[at : at + 16, 256:320] = block[48:64, 0:64]
        left[at + 16 : at + 24, 256:320] = block[48:56, 64:128]

    def place_weighted(base, ee):
        for s in range(4):
            at = (base + s) * 24
            right[at : at + 24, :] = wo_ref[s * 8 + lax.rem(ee + 4, 8)].astype(F32)[0:24]

    def product(half):
        rows = slice(half * 384, (half + 1) * 384)
        return lax.dot_general(
            left[rows].astype(BF16),
            right[rows].astype(BF16),
            (((0,), (0,)), ((), ())),
            preferred_element_type=F32,
        )

    for s in range(4):
        copy(t_buf, r_ref.at[e, s], ts.at[s], tr.at[s], (b, other)).wait_recv()
        for xx in x_order:
            along_x(e, x, xx, s).start()
        along_core(e, s).start()
        place(0, e, s)
    for s in range(4):
        for i, xx in enumerate(x_order):
            ee = xx * 2 + c
            along_x(ee, xx, xx, s).wait_recv()
            along_core(ee, s).start()
            place(4 + 4 * i, ee, s)
    all_panels().wait_recv()
    for i, xx in enumerate([x] + x_order):
        place_weighted(4 * i, xx * 2 + c)
        place_weighted(16 + 4 * i, xx * 2 + 1 - c)
    for zz in z_order:
        to_rows(zz).wait_send()
    all_panels().wait_send()
    chi = product(0)
    for i, xx in enumerate([x] + x_order):
        for s in range(4):
            along_core(xx * 2 + 1 - c, s).wait_recv()
            place(16 + 4 * i, xx * 2 + 1 - c, s)
    out_ref[...] = chi + product(1)
    for s in range(4):
        for xx in x_order:
            along_x(e, x, xx, s).wait_send()
        for xx in [x] + x_order:
            along_core(xx * 2 + c, s).wait_send()


def per_device(valence, conduction, owners, val_energy, cond_energy, gvec_index, ztab, ytab, xtab):
    dma = pltpu.SemaphoreType.DMA
    piece = (NV, NB, 16, 128)
    tile = (64, 128)
    return pl.pallas_call(
        main_kernel,
        out_shape=pltpu.VMEM((NGD, PANEL), F32),
        in_specs=[pl.BlockSpec(memory_space=pl.ANY)] * 9,
        out_specs=VMEM,
        scratch_shapes=[
            pltpu.SMEM((NV,), jnp.int32),
            pltpu.VMEM((NGD,), jnp.int32),
            pltpu.VMEM(piece, BF16),
            pltpu.VMEM((NC, 4, NGRID, NGRID), BF16),
            pltpu.SMEM((NV,), F32),
            pltpu.SMEM((NC,), F32),
            pltpu.VMEM(ztab.shape, BF16),
            pltpu.VMEM(ytab.shape, BF16),
            pltpu.VMEM(xtab.shape[1:], BF16),
            pltpu.VMEM(piece, BF16),
            pltpu.VMEM(piece, BF16),
            pltpu.VMEM(piece, BF16),
            pltpu.VMEM((NGA, 1, NGD), jnp.int32),
            pltpu.VMEM((NGA, 128, NGD), BF16),
            pltpu.VMEM((NGA, 8 * NF, NGD), F32),
            pltpu.VMEM((2, 2, 2 * NGRID, 2 * NGRID), BF16),
            pltpu.VMEM((4 * NF * KB, 128), F32),
            pltpu.VMEM((2, 4, 4) + tile, F32),
            pltpu.VMEM((4, 4) + tile, F32),
            pltpu.VMEM((4, 4) + tile, F32),
            pltpu.VMEM((4, 4) + tile, F32),
            pltpu.VMEM((4,) + tile, F32),
            pltpu.VMEM((4,) + tile, F32),
            pltpu.VMEM(tile, BF16),
            pltpu.VMEM((32, PANEL), BF16),
            pltpu.VMEM((8, 4) + tile, BF16),
            pltpu.VMEM((NB, 32, PANEL), BF16),
            pltpu.VMEM((NB * 24, NGD), F32),
            pltpu.VMEM((NB * 24, PANEL), F32),
            pltpu.SemaphoreType.REGULAR,
            dma((9,)),
            dma((NV,)),
            dma((NV,)),
            dma((NV,)),
            dma((NV,)),
            dma((4,)),
            dma((4,)),
            dma((4,)),
            dma((4,)),
            dma,
            dma,
            dma((4,)),
            dma((4,)),
            dma((4, 4)),
            dma((4, 4)),
            dma((4,)),
            dma((4,)),
            dma((4,)),
            dma((4,)),
            dma,
            dma,
            dma((4, 4)),
            dma((4, 4)),
            dma((8, 4)),
            dma((8, 4)),
        ],
        compiler_params=pltpu.CompilerParams(collective_id=1, has_side_effects=True),
    )(
        owners, val_energy, cond_energy, gvec_index, valence.reshape(piece), conduction, ztab, ytab, xtab
    )


def solution(mesh):
    ztab, ytab, xtab = (jnp.asarray(t) for t in tables())

    def step(valence, conduction, owners, val_energy, cond_energy, gvec_index):
        return jax.shard_map(
            per_device,
            mesh=mesh,
            in_specs=(
                P("band", None, "ga", None, None),
                P("band", "ga", None, None),
                P(),
                P(),
                P("band"),
                P("ga"),
                P(),
                P(),
                P(),
            ),
            out_specs=P("band", "ga"),
            check_vma=False,
        )(valence, conduction, owners, val_energy, cond_energy, gvec_index, ztab, ytab, xtab)

    return step
```
